256 devices in a mesh: plan: 32 (over x, y, core), draw: 8 (over z).
Axes of the slice: x: 4, y: 4, z: 8, core: 2. Of those that a mesh axis runs over, the one named last changes fastest.
Arguments:
- design: float32 [256, 128, 1024], P('plan', None, 'draw'), may hold values from 0 to 1
- class_ids: int32 [256, 128, 1024], P('plan', None, 'draw'), may hold values from 0 to 7
- class_radii: float32 [8, 3], replicated, may hold values from 0.5 to 16
- sensitivity: float32 [256, 128, 1024], P('plan', None, 'draw'), may hold values from -6 to 6
- row_patch: int32 [32, 8, 1024], P('plan', 'draw'), may hold values from 0 to 16383, as said below
Outputs:
- cast_density: float32 [256, 128, 1024], P('plan', None, 'draw')
- filtered_sens: float32 [256, 128, 1024], P('plan', None, 'draw')
- patch_sens: float32 [16384, 1024], P('plan', 'draw')
The draws below stay inside these ranges and needn't reach their ends.
Inputs may be any that keep to these rules, and one draw needn't show every extreme that they name: `row_patch`: patch q belongs to plan tile q // 512. Of the rows of one device, at most 128 belong to the patches of any one plan tile; in every draw slab one plan tile gets exactly 128 rows from every device of that slab.
All inputs are finite; a program needn't handle non-finite values.
Results may differ from the reference program's by a relative error of at most 0.00017.
Values sent between devices are 32-bit elements; how exact they have to be, the bound alone decides.
A program may use at most 64 MiB of HBM per device.

```python
import math
import jax
import jax.numpy as jnp
from jax import lax

CX = 8
NY = 128
CZ = 128
PATCH_DEV = 512
SWEEPS = 16
NCLS = 8
NX = 256
NZ = 1024
PATCHES = 16384
N_PLAN = 32
N_DRAW = 8


def draw_row_patch(key, part):
    rows = CX * NY
    cap = 4 * rows // N_PLAN
    light = rows - cap - cap // 2

    def one(device):
        slab = device % N_DRAW
        heavy = jax.random.randint(jax.random.fold_in(jax.random.fold_in(key, 11), slab), (), 0, N_PLAN)
        dev_key = jax.random.fold_in(key, 1000 + device)
        key_a, key_b, key_c, key_d = jax.random.split(dev_key, 4)
        spread = jax.random.randint(key_a, (cap // 2,), 1, N_PLAN)
        start = jax.random.randint(key_b, (), 0, N_PLAN - 1)
        cycle = 1 + (start + jnp.arange(light, dtype=jnp.int32)) % (N_PLAN - 1)
        offsets = jnp.concatenate([jnp.zeros((cap,), jnp.int32), spread.astype(jnp.int32), cycle.astype(jnp.int32)])
        owners = (heavy + offsets) % N_PLAN
        owners = owners[jax.random.permutation(key_c, rows)]
        slot_patch = jax.random.randint(key_d, (rows,), 0, PATCH_DEV)
        return (owners * PATCH_DEV + slot_patch).astype(jnp.int32)
    drawn = jax.vmap(one)(jnp.arange(N_PLAN * N_DRAW, dtype=jnp.int32))
    return drawn.reshape(N_PLAN, N_DRAW, rows)


def place_ends(result, key, least, largest):
    longest = result.shape.index(max(result.shape))
    spots = []
    for shift in (0, 1):
        where = [jax.random.randint(jax.random.fold_in(key, axis), (), 0, length) for axis, length in enumerate(result.shape)]
        where[longest] = (where[longest] + shift) % result.shape[longest]
        spots.append(tuple(where))
    return result.at[spots[0]].set(least).at[spots[1]].set(largest)


def shard_levels(key, shape, shards, low, largest):
    factor_of, own = 1.0, jax.random.fold_in(key, 6)
    for axis_at, blocks in shards:
        steps = jnp.exp(jax.random.uniform(jax.random.fold_in(own, axis_at), (blocks,), jnp.float32, low / len(shards), largest / len(shards)))
        factor_of = factor_of * jnp.repeat(steps, shape[axis_at] // blocks).reshape([-1 if axis == axis_at else 1 for axis in range(len(shape))])
    return factor_of


def scatter_about(stream_key, shape, deviation, bound, shards=(), held_as=jnp.bfloat16):
    loudness = shard_levels(stream_key, shape, shards, -0.22, 0.18) if shards else 1.0
    values = jax.random.normal(stream_key, shape, jnp.float32) * deviation * loudness
    return jnp.minimum(jnp.maximum(values, -bound), bound).astype(held_as)


def setup_inputs(seed: int = 0) -> dict:
    arg_keys = jax.random.split(jax.random.key(seed), 6)
    return {
        "design": jnp.clip(1.0 * jax.random.uniform(arg_keys[0], (NX, NY, NZ), jnp.float32) ** shard_levels(arg_keys[0], (NX, NY, NZ), ((0, 32), (2, 8)), -0.2, 0.2), 0.0, 1.0),
        "class_ids": place_ends(jax.random.randint(arg_keys[1], (NX, NY, NZ), 0, NCLS), jax.random.fold_in(arg_keys[1], 1), 0, NCLS - 1).astype(jnp.int32),
        "class_radii": jnp.clip(jnp.exp(jax.random.uniform(arg_keys[2], (NCLS, 3), jnp.float32, math.log(0.5), math.log(16.0))), 0.5, 16.0),
        "sensitivity": scatter_about(arg_keys[3], (NX, NY, NZ), 1.0, 6.0, ((0, 32), (2, 8)), jnp.float32),
        "row_patch": draw_row_patch(jax.random.fold_in(arg_keys[5], 71), 0),
    }


BETA = 8.0
ETA = 0.5
RMIN = 0.2
POWER = 6.0


def coefficients(class_ids, class_radii):
    coef_x = jnp.zeros(class_ids.shape, jnp.float32)
    coef_y = jnp.zeros(class_ids.shape, jnp.float32)
    coef_z = jnp.zeros(class_ids.shape, jnp.float32)
    for level in range(class_radii.shape[0]):
        hit = class_ids == level
        coef_x = jnp.where(hit, class_radii[level, 0], coef_x)
        coef_y = jnp.where(hit, class_radii[level, 1], coef_y)
        coef_z = jnp.where(hit, class_radii[level, 2], coef_z)
    return coef_x, coef_y, coef_z


def relax(padded, coef_x, coef_y, coef_z, inv_diag, source):
    along_x = padded[2:, 1:-1, 1:-1] + padded[:-2, 1:-1, 1:-1]
    along_y = padded[1:-1, 2:, 1:-1] + padded[1:-1, :-2, 1:-1]
    along_z = padded[1:-1, 1:-1, 2:] + padded[1:-1, 1:-1, :-2]
    return (source + coef_x * along_x + coef_y * along_y + coef_z * along_z) * inv_diag


def smooth(source, coef_x, coef_y, coef_z, inv_diag):
    def sweep(index, field):
        return relax(jnp.pad(field, 1), coef_x, coef_y, coef_z, inv_diag, source)
    return lax.fori_loop(0, SWEEPS, sweep, source)


def reference(design, class_ids, class_radii, sensitivity, row_patch):
    coef_x, coef_y, coef_z = coefficients(class_ids, class_radii)
    inv_diag = 1.0 / (1.0 + 2.0 * (coef_x + coef_y + coef_z))
    filtered = smooth(design, coef_x, coef_y, coef_z, inv_diag)
    denom = jnp.tanh(jnp.float32(BETA * ETA)) + jnp.tanh(jnp.float32(BETA * (1.0 - ETA)))
    steep = jnp.tanh(BETA * (filtered - ETA))
    projected = RMIN + (1.0 - RMIN) * (jnp.tanh(jnp.float32(BETA * ETA)) + steep) / denom
    prefix = jnp.cumsum(jnp.power(projected, POWER), axis=2)
    cast_density = jnp.power(prefix, 1.0 / POWER)
    weighted = sensitivity * jnp.power(prefix, (1.0 - POWER) / POWER)
    suffix = jnp.flip(jnp.cumsum(jnp.flip(weighted, 2), axis=2), 2)
    chained = jnp.power(projected, POWER - 1.0) * suffix * (1.0 - RMIN) * BETA * (1.0 - steep * steep) / denom
    filtered_sens = smooth(chained, coef_x, coef_y, coef_z, inv_diag)
    row_data = filtered_sens.reshape(N_PLAN, CX, NY, N_DRAW, CZ).transpose(0, 3, 1, 2, 4)
    row_data = row_data.reshape(N_PLAN, N_DRAW, CX * NY, CZ)
    columns = []
    for slab in range(N_DRAW):
        summed = jax.ops.segment_sum(row_data[:, slab].reshape(-1, CZ), row_patch[:, slab].reshape(-1), num_segments=PATCHES)
        columns.append(summed)
    patch_sens = 0.25 * jnp.concatenate(columns, axis=1)
    return cast_density, filtered_sens, patch_sens
```

```python
import functools

import jax
import jax.numpy as jnp
from jax import lax
from jax.experimental import pallas as pl
from jax.experimental.pallas import tpu as pltpu
from jax.sharding import PartitionSpec as P

PATCH_DEV = 512
SWEEPS = 16
HALO = 8

BETA = 8.0
ETA = 0.5
RMIN = 0.2
POWER = 6.0

MESH = pl.DeviceIdType.MESH


def entering(part, axis, combine, identity, reverse):
    count = lax.axis_size(axis)
    place = lax.axis_index(axis)
    ahead = count - 1 - place if reverse else place
    gathered = lax.all_gather(part, axis)
    state = jnp.zeros_like(part) + jnp.asarray(identity, part.dtype)

    def one(step, state):
        source = count - 1 - step if reverse else step
        return combine(state, lax.dynamic_index_in_dim(gathered, source, 0, False))

    return lax.fori_loop(0, ahead, one, state)


def coefficients(class_ids, class_radii):
    coef_x = jnp.zeros(class_ids.shape, jnp.float32)
    coef_y = jnp.zeros(class_ids.shape, jnp.float32)
    coef_z = jnp.zeros(class_ids.shape, jnp.float32)
    for level in range(class_radii.shape[0]):
        hit = class_ids == level
        coef_x = jnp.where(hit, class_radii[level, 0], coef_x)
        coef_y = jnp.where(hit, class_radii[level, 1], coef_y)
        coef_z = jnp.where(hit, class_radii[level, 2], coef_z)
    return (coef_x, coef_y, coef_z)


def filter_kernel(n_plan, n_draw, src_ref, cx_ref, cy_ref, cz_ref, inv_ref, out_ref, field, send_sem, recv_sem):
    planes, depth, width = src_ref.shape
    p = lax.axis_index("plan")
    d = lax.axis_index("draw")
    has_l = p > 0
    has_r = p < n_plan - 1
    has_b = d > 0
    has_a = d < n_draw - 1
    lo = HALO
    hi = HALO + depth

    field[...] = jnp.zeros_like(field)
    for i in range(planes):
        field[0, i + 1, pl.ds(lo, depth), :] = src_ref[i]

    barrier = pltpu.get_barrier_semaphore()
    neighbours = ((has_l, (p - 1, d)), (has_r, (p + 1, d)), (has_b, (p, d - 1)), (has_a, (p, d + 1)))
    for cond, dev in neighbours:
        @pl.when(cond)
        def _():
            pl.semaphore_signal(barrier, 1, device_id=dev, device_id_type=MESH)
    peers = sum(cond.astype(jnp.int32) for cond, _ in neighbours)
    pl.semaphore_wait(barrier, peers)

    def copies(s):
        to_l = pltpu.make_async_remote_copy(
            field.at[s, 1, pl.ds(lo, depth), :], field.at[s, planes + 1, pl.ds(lo, depth), :],
            send_sem.at[s, 0], recv_sem.at[s, 0], device_id=(p - 1, d), device_id_type=MESH)
        to_r = pltpu.make_async_remote_copy(
            field.at[s, planes, pl.ds(lo, depth), :], field.at[s, 0, pl.ds(lo, depth), :],
            send_sem.at[s, 1], recv_sem.at[s, 1], device_id=(p + 1, d), device_id_type=MESH)
        to_b = pltpu.make_async_remote_copy(
            field.at[s, pl.ds(1, planes), pl.ds(lo, HALO), :], field.at[s, pl.ds(1, planes), pl.ds(hi, HALO), :],
            send_sem.at[s, 2], recv_sem.at[s, 2], device_id=(p, d - 1), device_id_type=MESH)
        to_a = pltpu.make_async_remote_copy(
            field.at[s, pl.ds(1, planes), pl.ds(hi - HALO, HALO), :], field.at[s, pl.ds(1, planes), pl.ds(0, HALO), :],
            send_sem.at[s, 3], recv_sem.at[s, 3], device_id=(p, d + 1), device_id_type=MESH)
        return ((to_l, has_l, has_r), (to_r, has_r, has_l), (to_b, has_b, has_a), (to_a, has_a, has_b))

    def exchange(s):
        group = copies(s)
        for copy, send, _ in group:
            @pl.when(send)
            def _():
                copy.start()
        for copy, send, recv in group:
            @pl.when(send)
            def _():
                copy.wait_send()

            @pl.when(recv)
            def _():
                copy.wait_recv()

    lane = lax.broadcasted_iota(jnp.int32, (depth, width), 1)

    def sweep(s, last):
        t = 1 - s
        for i in range(planes):
            c = field[s, i + 1, pl.ds(lo, depth), :]
            zm = field[s, i + 1, pl.ds(lo - 1, depth), :]
            zp = field[s, i + 1, pl.ds(lo + 1, depth), :]
            xm = field[s, i, pl.ds(lo, depth), :]
            xp = field[s, i + 2, pl.ds(lo, depth), :]
            ym = jnp.where(lane == 0, 0.0, pltpu.roll(c, 1, 1))
            yp = jnp.where(lane == width - 1, 0.0, pltpu.roll(c, width - 1, 1))
            new = (src_ref[i] + cx_ref[i] * (xm + xp) + cy_ref[i] * (ym + yp) + cz_ref[i] * (zm + zp)) * inv_ref[i]
            if last:
                out_ref[i] = new
            else:
                field[t, i + 1, pl.ds(lo, depth), :] = new

    exchange(0)

    def pair(k, carry):
        sweep(0, False)
        exchange(1)
        sweep(1, False)
        exchange(0)
        return carry

    lax.fori_loop(0, SWEEPS // 2 - 1, pair, 0)
    sweep(0, False)
    exchange(1)
    sweep(1, True)


def smooth_each(source, coef_x, coef_y, coef_z, inv_diag, n_plan, n_draw, kid):
    planes, depth, width = source.shape
    vmem = pl.BlockSpec(memory_space=pltpu.VMEM)
    return pl.pallas_call(
        functools.partial(filter_kernel, n_plan, n_draw),
        out_shape=jax.ShapeDtypeStruct(source.shape, jnp.float32),
        in_specs=[vmem] * 5,
        out_specs=vmem,
        scratch_shapes=[
            pltpu.VMEM((2, planes + 2, depth + 2 * HALO, width), jnp.float32),
            pltpu.SemaphoreType.DMA((2, 4)),
            pltpu.SemaphoreType.DMA((2, 4)),
        ],
        compiler_params=pltpu.CompilerParams(collective_id=kid, has_side_effects=True),
    )(source, coef_x, coef_y, coef_z, inv_diag)


def per_device(n_plan, n_draw, design, class_ids, class_radii, sensitivity, row_patch):
    design_t = jnp.swapaxes(design, 1, 2)
    ids_t = jnp.swapaxes(class_ids, 1, 2)
    sens_t = jnp.swapaxes(sensitivity, 1, 2)
    coef_x, coef_y, coef_z = coefficients(ids_t, class_radii)
    inv_diag = 1.0 / (1.0 + 2.0 * (coef_x + coef_y + coef_z))
    filtered = smooth_each(design_t, coef_x, coef_y, coef_z, inv_diag, n_plan, n_draw, 0)
    denom = jnp.tanh(jnp.float32(BETA * ETA)) + jnp.tanh(jnp.float32(BETA * (1.0 - ETA)))
    steep = jnp.tanh(BETA * (filtered - ETA))
    projected = RMIN + (1.0 - RMIN) * (jnp.tanh(jnp.float32(BETA * ETA)) + steep) / denom
    running = jnp.cumsum(jnp.power(projected, POWER), axis=1)
    totals = running[:, -1, :]
    carried = entering(
        totals, "draw", lambda first, second: first + second, jnp.zeros_like(totals), False
    )
    prefix = running + carried[:, None, :]
    cast_density = jnp.power(prefix, 1.0 / POWER)
    weighted = sens_t * jnp.power(prefix, (1.0 - POWER) / POWER)
    backward = jnp.flip(jnp.cumsum(jnp.flip(weighted, 1), axis=1), 1)
    rests = backward[:, 0, :]
    below = entering(
        rests, "draw", lambda first, second: first + second, jnp.zeros_like(rests), True
    )
    suffix = backward + below[:, None, :]
    chained = (
        jnp.power(projected, POWER - 1.0)
        * suffix
        * (1.0 - RMIN)
        * BETA
        * (1.0 - steep * steep)
        / denom
    )
    filtered_sens_t = smooth_each(chained, coef_x, coef_y, coef_z, inv_diag, n_plan, n_draw, 1)
    filtered_sens = jnp.swapaxes(filtered_sens_t, 1, 2)
    cast_density = jnp.swapaxes(cast_density, 1, 2)
    depth = filtered_sens.shape[2]
    row_count = filtered_sens.shape[0] * filtered_sens.shape[1]
    tiles = lax.axis_size("plan")
    capacity = 4 * row_count // tiles
    row_data = filtered_sens.reshape(row_count, depth)
    patch_ids = row_patch.reshape(row_count)
    owners = patch_ids // PATCH_DEV
    slot_patch = patch_ids - owners * PATCH_DEV
    onehot = (owners[:, None] == jnp.arange(tiles, dtype=jnp.int32)[None, :]).astype(jnp.int32)
    ranking = jnp.sum(jnp.cumsum(onehot, axis=0) * onehot, axis=1) - 1
    position = owners * capacity + ranking
    sendbuf = jnp.zeros((tiles * capacity, depth), jnp.float32).at[position].set(row_data)
    send_ids = (
        jnp.full((tiles * capacity,), float(PATCH_DEV), jnp.float32)
        .at[position]
        .set(slot_patch.astype(jnp.float32))
    )
    arrived, arrived_ids = (
        lax.all_to_all(
            sendbuf.reshape(tiles, capacity, depth), "plan", split_axis=0, concat_axis=0, tiled=True
        ),
        lax.all_to_all(
            send_ids.reshape(tiles, capacity), "plan", split_axis=0, concat_axis=0, tiled=True
        ),
    )
    summed = jax.ops.segment_sum(
        arrived.reshape(tiles * capacity, depth),
        arrived_ids.reshape(tiles * capacity).astype(jnp.int32),
        num_segments=PATCH_DEV + 1,
    )
    patch_sens = 0.25 * summed[:PATCH_DEV]
    return (cast_density, filtered_sens, patch_sens)


def solution(mesh):
    in_specs = (
        P("plan", None, "draw"),
        P("plan", None, "draw"),
        P(),
        P("plan", None, "draw"),
        P("plan", "draw", None),
    )
    out_specs = (P("plan", None, "draw"), P("plan", None, "draw"), P("plan", "draw"))
    return jax.shard_map(
        functools.partial(per_device, mesh.shape["plan"], mesh.shape["draw"]),
        mesh=mesh, in_specs=in_specs, out_specs=out_specs, check_vma=False
    )
```

```python
import functools

import jax
import jax.numpy as jnp
from jax import lax
from jax.experimental import pallas as pl
from jax.experimental.pallas import tpu as pltpu
from jax.sharding import PartitionSpec as P

PATCH_DEV = 512
SWEEPS = 16
HALO = 8

BETA = 8.0
ETA = 0.5
RMIN = 0.2
POWER = 6.0

MESH = pl.DeviceIdType.MESH


def scan_kernel(n_draw, reverse, part_ref, out_ref, held, send_sem, recv_sem):
    p = lax.axis_index("plan")
    d = lax.axis_index("draw")
    held[...] = jnp.zeros_like(held)
    barrier = pltpu.get_barrier_semaphore()
    for e in range(n_draw):
        @pl.when(d != e)
        def _():
            pl.semaphore_signal(barrier, 1, device_id=(p, e), device_id_type=MESH)
    pl.semaphore_wait(barrier, n_draw - 1)

    def later(e):
        return e < d if reverse else e > d

    def earlier(e):
        return e > d if reverse else e < d

    sends = []
    for e in range(n_draw):
        copy = pltpu.make_async_remote_copy(
            part_ref, held.at[d], send_sem.at[e], recv_sem.at[d], device_id=(p, e), device_id_type=MESH)
        sends.append(copy)

        @pl.when(later(e))
        def _():
            copy.start()
    for e in range(n_draw):
        incoming = pltpu.make_async_remote_copy(
            part_ref, held.at[e], send_sem.at[e], recv_sem.at[e], device_id=(p, e), device_id_type=MESH)

        @pl.when(later(e))
        def _():
            sends[e].wait_send()

        @pl.when(earlier(e))
        def _():
            incoming.wait_recv()
    total = held[0]
    for e in range(1, n_draw):
        total = total + held[e]
    out_ref[...] = total


def entering(part, n_draw, reverse, kid):
    vmem = pl.BlockSpec(memory_space=pltpu.VMEM)
    return pl.pallas_call(
        functools.partial(scan_kernel, n_draw, reverse),
        out_shape=jax.ShapeDtypeStruct(part.shape, jnp.float32),
        in_specs=[vmem],
        out_specs=vmem,
        scratch_shapes=[
            pltpu.VMEM((n_draw,) + part.shape, jnp.float32),
            pltpu.SemaphoreType.DMA((n_draw,)),
            pltpu.SemaphoreType.DMA((n_draw,)),
        ],
        compiler_params=pltpu.CompilerParams(collective_id=kid, has_side_effects=True),
    )(part)


def filter_kernel(n_plan, n_draw, src_ref, ids_ref, radii_ref, out_ref, field, cx_ref, cy_ref, cz_ref, inv_ref,
                  send_sem, recv_sem):
    planes, depth, width = src_ref.shape
    for i in range(planes):
        cls = ids_ref[i]
        cx = jnp.zeros((depth, width), jnp.float32)
        cy = jnp.zeros((depth, width), jnp.float32)
        cz = jnp.zeros((depth, width), jnp.float32)
        for level in range(radii_ref.shape[0]):
            hit = cls == level
            cx = jnp.where(hit, radii_ref[level, 0], cx)
            cy = jnp.where(hit, radii_ref[level, 1], cy)
            cz = jnp.where(hit, radii_ref[level, 2], cz)
        cx_ref[i] = cx
        cy_ref[i] = cy
        cz_ref[i] = cz
        inv_ref[i] = 1.0 / (1.0 + 2.0 * (cx + cy + cz))
    p = lax.axis_index("plan")
    d = lax.axis_index("draw")
    has_l = p > 0
    has_r = p < n_plan - 1
    has_b = d > 0
    has_a = d < n_draw - 1
    lo = HALO
    hi = HALO + depth

    field[...] = jnp.zeros_like(field)
    for i in range(planes):
        field[0, i + 1, pl.ds(lo, depth), :] = src_ref[i]

    barrier = pltpu.get_barrier_semaphore()
    neighbours = ((has_l, (p - 1, d)), (has_r, (p + 1, d)), (has_b, (p, d - 1)), (has_a, (p, d + 1)))
    for cond, dev in neighbours:
        @pl.when(cond)
        def _():
            pl.semaphore_signal(barrier, 1, device_id=dev, device_id_type=MESH)
    peers = sum(cond.astype(jnp.int32) for cond, _ in neighbours)
    pl.semaphore_wait(barrier, peers)

    def copies(s):
        to_l = pltpu.make_async_remote_copy(
            field.at[s, 1, pl.ds(lo, depth), :], field.at[s, planes + 1, pl.ds(lo, depth), :],
            send_sem.at[s, 0], recv_sem.at[s, 0], device_id=(p - 1, d), device_id_type=MESH)
        to_r = pltpu.make_async_remote_copy(
            field.at[s, planes, pl.ds(lo, depth), :], field.at[s, 0, pl.ds(lo, depth), :],
            send_sem.at[s, 1], recv_sem.at[s, 1], device_id=(p + 1, d), device_id_type=MESH)
        to_b = pltpu.make_async_remote_copy(
            field.at[s, pl.ds(1, planes), pl.ds(lo, HALO), :], field.at[s, pl.ds(1, planes), pl.ds(hi, HALO), :],
            send_sem.at[s, 2], recv_sem.at[s, 2], device_id=(p, d - 1), device_id_type=MESH)
        to_a = pltpu.make_async_remote_copy(
            field.at[s, pl.ds(1, planes), pl.ds(hi - HALO, HALO), :], field.at[s, pl.ds(1, planes), pl.ds(0, HALO), :],
            send_sem.at[s, 3], recv_sem.at[s, 3], device_id=(p, d + 1), device_id_type=MESH)
        return ((to_l, has_l, has_r), (to_r, has_r, has_l), (to_b, has_b, has_a), (to_a, has_a, has_b))

    def exchange(s):
        group = copies(s)
        for copy, send, _ in group:
            @pl.when(send)
            def _():
                copy.start()
        for copy, send, recv in group:
            @pl.when(send)
            def _():
                copy.wait_send()

            @pl.when(recv)
            def _():
                copy.wait_recv()

    lane = lax.broadcasted_iota(jnp.int32, (depth, width), 1)

    def sweep(s, last):
        t = 1 - s
        for i in range(planes):
            c = field[s, i + 1, pl.ds(lo, depth), :]
            zm = field[s, i + 1, pl.ds(lo - 1, depth), :]
            zp = field[s, i + 1, pl.ds(lo + 1, depth), :]
            xm = field[s, i, pl.ds(lo, depth), :]
            xp = field[s, i + 2, pl.ds(lo, depth), :]
            ym = jnp.where(lane == 0, 0.0, pltpu.roll(c, 1, 1))
            yp = jnp.where(lane == width - 1, 0.0, pltpu.roll(c, width - 1, 1))
            new = (src_ref[i] + cx_ref[i] * (xm + xp) + cy_ref[i] * (ym + yp) + cz_ref[i] * (zm + zp)) * inv_ref[i]
            if last:
                out_ref[i] = new
            else:
                field[t, i + 1, pl.ds(lo, depth), :] = new

    exchange(0)

    def pair(k, carry):
        sweep(0, False)
        exchange(1)
        sweep(1, False)
        exchange(0)
        return carry

    lax.fori_loop(0, SWEEPS // 2 - 1, pair, 0)
    sweep(0, False)
    exchange(1)
    sweep(1, True)


def smooth_each(source, class_ids, class_radii, n_plan, n_draw, kid):
    planes, depth, width = source.shape
    vmem = pl.BlockSpec(memory_space=pltpu.VMEM)
    smem = pl.BlockSpec(memory_space=pltpu.SMEM)
    return pl.pallas_call(
        functools.partial(filter_kernel, n_plan, n_draw),
        out_shape=jax.ShapeDtypeStruct(source.shape, jnp.float32),
        in_specs=[vmem, vmem, smem],
        out_specs=vmem,
        scratch_shapes=[
            pltpu.VMEM((2, planes + 2, depth + 2 * HALO, width), jnp.float32),
            pltpu.VMEM(source.shape, jnp.float32),
            pltpu.VMEM(source.shape, jnp.float32),
            pltpu.VMEM(source.shape, jnp.float32),
            pltpu.VMEM(source.shape, jnp.float32),
            pltpu.SemaphoreType.DMA((2, 4)),
            pltpu.SemaphoreType.DMA((2, 4)),
        ],
        compiler_params=pltpu.CompilerParams(collective_id=kid, has_side_effects=True),
    )(source, class_ids, class_radii)


def per_device(n_plan, n_draw, design, class_ids, class_radii, sensitivity, row_patch):
    design_t = jnp.swapaxes(design, 1, 2)
    ids_t = jnp.swapaxes(class_ids, 1, 2)
    sens_t = jnp.swapaxes(sensitivity, 1, 2)
    filtered = smooth_each(design_t, ids_t, class_radii, n_plan, n_draw, 0)
    denom = jnp.tanh(jnp.float32(BETA * ETA)) + jnp.tanh(jnp.float32(BETA * (1.0 - ETA)))
    steep = jnp.tanh(BETA * (filtered - ETA))
    projected = RMIN + (1.0 - RMIN) * (jnp.tanh(jnp.float32(BETA * ETA)) + steep) / denom
    running = jnp.cumsum(jnp.power(projected, POWER), axis=1)
    totals = running[:, -1, :]
    carried = entering(totals, n_draw, False, 2)
    prefix = running + carried[:, None, :]
    cast_density = jnp.power(prefix, 1.0 / POWER)
    weighted = sens_t * jnp.power(prefix, (1.0 - POWER) / POWER)
    backward = lax.cumsum(weighted, axis=1, reverse=True)
    rests = backward[:, 0, :]
    below = entering(rests, n_draw, True, 3)
    suffix = backward + below[:, None, :]
    chained = (
        jnp.power(projected, POWER - 1.0)
        * suffix
        * (1.0 - RMIN)
        * BETA
        * (1.0 - steep * steep)
        / denom
    )
    filtered_sens_t = smooth_each(chained, ids_t, class_radii, n_plan, n_draw, 1)
    filtered_sens = jnp.swapaxes(filtered_sens_t, 1, 2)
    cast_density = jnp.swapaxes(cast_density, 1, 2)
    depth = filtered_sens.shape[2]
    row_count = filtered_sens.shape[0] * filtered_sens.shape[1]
    tiles = lax.axis_size("plan")
    capacity = 4 * row_count // tiles
    row_data = filtered_sens.reshape(row_count, depth)
    patch_ids = row_patch.reshape(row_count)
    owners = patch_ids // PATCH_DEV
    slot_patch = patch_ids - owners * PATCH_DEV
    onehot = (owners[:, None] == jnp.arange(tiles, dtype=jnp.int32)[None, :]).astype(jnp.bfloat16)
    rows = jnp.arange(row_count, dtype=jnp.int32)
    upto = (rows[None, :] <= rows[:, None]).astype(jnp.bfloat16)
    counted = jnp.dot(upto, onehot, preferred_element_type=jnp.float32)
    ranking = jnp.sum(counted * onehot.astype(jnp.float32), axis=1).astype(jnp.int32) - 1
    position = owners * capacity + ranking
    source_row = jnp.full((tiles * capacity,), row_count, jnp.int32).at[position].set(rows)
    padded_rows = jnp.concatenate([row_data, jnp.zeros((1, depth), jnp.float32)], axis=0)
    padded_ids = jnp.concatenate([slot_patch.astype(jnp.float32), jnp.full((1,), float(PATCH_DEV), jnp.float32)])
    sendbuf = jnp.take(padded_rows, source_row, axis=0)
    send_ids = jnp.take(padded_ids, source_row, axis=0)
    arrived, arrived_ids = (
        lax.all_to_all(
            sendbuf.reshape(tiles, capacity, depth), "plan", split_axis=0, concat_axis=0, tiled=True
        ),
        lax.all_to_all(
            send_ids.reshape(tiles, capacity), "plan", split_axis=0, concat_axis=0, tiled=True
        ),
    )
    picks = (
        jnp.arange(PATCH_DEV, dtype=jnp.int32)[:, None] == arrived_ids.reshape(1, tiles * capacity).astype(jnp.int32)
    ).astype(jnp.float32)
    summed = jnp.dot(picks, arrived.reshape(tiles * capacity, depth), precision=lax.Precision.HIGHEST,
                     preferred_element_type=jnp.float32)
    patch_sens = 0.25 * summed
    return (cast_density, filtered_sens, patch_sens)


def solution(mesh):
    in_specs = (
        P("plan", None, "draw"),
        P("plan", None, "draw"),
        P(),
        P("plan", None, "draw"),
        P("plan", "draw", None),
    )
    out_specs = (P("plan", None, "draw"), P("plan", None, "draw"), P("plan", "draw"))
    return jax.shard_map(
        functools.partial(per_device, mesh.shape["plan"], mesh.shape["draw"]),
        mesh=mesh, in_specs=in_specs, out_specs=out_specs, check_vma=False
    )
```

```python
import functools

import jax
import jax.numpy as jnp
from jax import lax
from jax.experimental import pallas as pl
from jax.experimental.pallas import tpu as pltpu
from jax.sharding import PartitionSpec as P

PATCH_DEV = 512
SWEEPS = 16
HALO = 8

BETA = 8.0
ETA = 0.5
RMIN = 0.2
POWER = 6.0

MESH = pl.DeviceIdType.MESH


def scan_kernel(n_draw, reverse, part_ref, out_ref, held, send_sem, recv_sem):
    p = lax.axis_index("plan")
    d = lax.axis_index("draw")
    held[...] = jnp.zeros_like(held)
    barrier = pltpu.get_barrier_semaphore()
    for e in range(n_draw):
        @pl.when(d != e)
        def _():
            pl.semaphore_signal(barrier, 1, device_id=(p, e), device_id_type=MESH)
    pl.semaphore_wait(barrier, n_draw - 1)

    def later(e):
        return e < d if reverse else e > d

    def earlier(e):
        return e > d if reverse else e < d

    sends = []
    for e in range(n_draw):
        copy = pltpu.make_async_remote_copy(
            part_ref, held.at[d], send_sem.at[e], recv_sem.at[d], device_id=(p, e), device_id_type=MESH)
        sends.append(copy)

        @pl.when(later(e))
        def _():
            copy.start()
    for e in range(n_draw):
        incoming = pltpu.make_async_remote_copy(
            part_ref, held.at[e], send_sem.at[e], recv_sem.at[e], device_id=(p, e), device_id_type=MESH)

        @pl.when(later(e))
        def _():
            sends[e].wait_send()

        @pl.when(earlier(e))
        def _():
            incoming.wait_recv()
    total = held[0]
    for e in range(1, n_draw):
        total = total + held[e]
    out_ref[...] = total


def entering(part, n_draw, reverse, kid):
    vmem = pl.BlockSpec(memory_space=pltpu.VMEM)
    return pl.pallas_call(
        functools.partial(scan_kernel, n_draw, reverse),
        out_shape=jax.ShapeDtypeStruct(part.shape, jnp.float32),
        in_specs=[vmem],
        out_specs=vmem,
        scratch_shapes=[
            pltpu.VMEM((n_draw,) + part.shape, jnp.float32),
            pltpu.SemaphoreType.DMA((n_draw,)),
            pltpu.SemaphoreType.DMA((n_draw,)),
        ],
        compiler_params=pltpu.CompilerParams(collective_id=kid, has_side_effects=True),
    )(part)


def filter_kernel(n_plan, n_draw, src_ref, ids_ref, radii_ref, out_ref, field, cx_ref, cy_ref, cz_ref, inv_ref,
                  send_sem, recv_sem):
    planes, depth, width = src_ref.shape
    for i in range(planes):
        cls = ids_ref[i]
        cx = jnp.zeros((depth, width), jnp.float32)
        cy = jnp.zeros((depth, width), jnp.float32)
        cz = jnp.zeros((depth, width), jnp.float32)
        for level in range(radii_ref.shape[0]):
            hit = cls == level
            cx = jnp.where(hit, radii_ref[level, 0], cx)
            cy = jnp.where(hit, radii_ref[level, 1], cy)
            cz = jnp.where(hit, radii_ref[level, 2], cz)
        cx_ref[i] = cx
        cy_ref[i] = cy
        cz_ref[i] = cz
        inv_ref[i] = 1.0 / (1.0 + 2.0 * (cx + cy + cz))
    p = lax.axis_index("plan")
    d = lax.axis_index("draw")
    has_l = p > 0
    has_r = p < n_plan - 1
    has_b = d > 0
    has_a = d < n_draw - 1
    lo = HALO
    hi = HALO + depth

    field[...] = jnp.zeros_like(field)
    for i in range(planes):
        field[0, i + 1, pl.ds(lo, depth), :] = src_ref[i]

    barrier = pltpu.get_barrier_semaphore()
    neighbours = ((has_l, (p - 1, d)), (has_r, (p + 1, d)), (has_b, (p, d - 1)), (has_a, (p, d + 1)))
    for cond, dev in neighbours:
        @pl.when(cond)
        def _():
            pl.semaphore_signal(barrier, 1, device_id=dev, device_id_type=MESH)
    peers = sum(cond.astype(jnp.int32) for cond, _ in neighbours)
    pl.semaphore_wait(barrier, peers)

    def copies(s):
        to_l = pltpu.make_async_remote_copy(
            field.at[s, 1, pl.ds(lo, depth), :], field.at[s, planes + 1, pl.ds(lo, depth), :],
            send_sem.at[s, 0], recv_sem.at[s, 0], device_id=(p - 1, d), device_id_type=MESH)
        to_r = pltpu.make_async_remote_copy(
            field.at[s, planes, pl.ds(lo, depth), :], field.at[s, 0, pl.ds(lo, depth), :],
            send_sem.at[s, 1], recv_sem.at[s, 1], device_id=(p + 1, d), device_id_type=MESH)
        to_b = pltpu.make_async_remote_copy(
            field.at[s, pl.ds(1, planes), pl.ds(lo, HALO), :], field.at[s, pl.ds(1, planes), pl.ds(hi, HALO), :],
            send_sem.at[s, 2], recv_sem.at[s, 2], device_id=(p, d - 1), device_id_type=MESH)
        to_a = pltpu.make_async_remote_copy(
            field.at[s, pl.ds(1, planes), pl.ds(hi - HALO, HALO), :], field.at[s, pl.ds(1, planes), pl.ds(0, HALO), :],
            send_sem.at[s, 3], recv_sem.at[s, 3], device_id=(p, d + 1), device_id_type=MESH)
        return ((to_l, has_l, has_r), (to_r, has_r, has_l), (to_b, has_b, has_a), (to_a, has_a, has_b))

    def exchange(s):
        group = copies(s)
        for copy, send, _ in group:
            @pl.when(send)
            def _():
                copy.start()
        for copy, send, recv in group:
            @pl.when(send)
            def _():
                copy.wait_send()

            @pl.when(recv)
            def _():
                copy.wait_recv()

    lane = lax.broadcasted_iota(jnp.int32, (depth, width), 1)

    def update(s, i, r0, rows, last):
        at = lo + r0
        c = field[s, i + 1, pl.ds(at, rows), :]
        zm = field[s, i + 1, pl.ds(at - 1, rows), :]
        zp = field[s, i + 1, pl.ds(at + 1, rows), :]
        xm = field[s, i, pl.ds(at, rows), :]
        xp = field[s, i + 2, pl.ds(at, rows), :]
        lanes = lane[:rows]
        ym = jnp.where(lanes == 0, 0.0, pltpu.roll(c, 1, 1))
        yp = jnp.where(lanes == width - 1, 0.0, pltpu.roll(c, width - 1, 1))
        part = pl.ds(r0, rows)
        new = (src_ref[i, part, :] + cx_ref[i, part, :] * (xm + xp) + cy_ref[i, part, :] * (ym + yp)
               + cz_ref[i, part, :] * (zm + zp)) * inv_ref[i, part, :]
        if last:
            out_ref[i, part, :] = new
        else:
            field[1 - s, i + 1, pl.ds(at, rows), :] = new

    def sweep_send(s):
        t = 1 - s
        group = copies(t)
        update(s, 0, 0, depth, False)
        update(s, planes - 1, 0, depth, False)
        for copy, send, _ in group[:2]:
            @pl.when(send)
            def _():
                copy.start()
        for i in range(1, planes - 1):
            update(s, i, 0, HALO, False)
            update(s, i, depth - HALO, HALO, False)
        for copy, send, _ in group[2:]:
            @pl.when(send)
            def _():
                copy.start()
        for i in range(1, planes - 1):
            update(s, i, HALO, depth - 2 * HALO, False)
        for copy, send, recv in group:
            @pl.when(send)
            def _():
                copy.wait_send()

            @pl.when(recv)
            def _():
                copy.wait_recv()

    exchange(0)

    def pair(k, carry):
        sweep_send(0)
        sweep_send(1)
        return carry

    lax.fori_loop(0, SWEEPS // 2 - 1, pair, 0)
    sweep_send(0)
    for i in range(planes):
        update(1, i, 0, depth, True)


def smooth_each(source, class_ids, class_radii, n_plan, n_draw, kid):
    planes, depth, width = source.shape
    vmem = pl.BlockSpec(memory_space=pltpu.VMEM)
    smem = pl.BlockSpec(memory_space=pltpu.SMEM)
    return pl.pallas_call(
        functools.partial(filter_kernel, n_plan, n_draw),
        out_shape=jax.ShapeDtypeStruct(source.shape, jnp.float32),
        in_specs=[vmem, vmem, smem],
        out_specs=vmem,
        scratch_shapes=[
            pltpu.VMEM((2, planes + 2, depth + 2 * HALO, width), jnp.float32),
            pltpu.VMEM(source.shape, jnp.float32),
            pltpu.VMEM(source.shape, jnp.float32),
            pltpu.VMEM(source.shape, jnp.float32),
            pltpu.VMEM(source.shape, jnp.float32),
            pltpu.SemaphoreType.DMA((2, 4)),
            pltpu.SemaphoreType.DMA((2, 4)),
        ],
        compiler_params=pltpu.CompilerParams(collective_id=kid, has_side_effects=True),
    )(source, class_ids, class_radii)


def per_device(n_plan, n_draw, design, class_ids, class_radii, sensitivity, row_patch):
    design_t = jnp.swapaxes(design, 1, 2)
    ids_t = jnp.swapaxes(class_ids, 1, 2)
    sens_t = jnp.swapaxes(sensitivity, 1, 2)
    filtered = smooth_each(design_t, ids_t, class_radii, n_plan, n_draw, 0)
    denom = jnp.tanh(jnp.float32(BETA * ETA)) + jnp.tanh(jnp.float32(BETA * (1.0 - ETA)))
    steep = jnp.tanh(BETA * (filtered - ETA))
    projected = RMIN + (1.0 - RMIN) * (jnp.tanh(jnp.float32(BETA * ETA)) + steep) / denom
    running = jnp.cumsum(jnp.power(projected, POWER), axis=1)
    totals = running[:, -1, :]
    carried = entering(totals, n_draw, False, 2)
    prefix = running + carried[:, None, :]
    cast_density = jnp.power(prefix, 1.0 / POWER)
    weighted = sens_t * jnp.power(prefix, (1.0 - POWER) / POWER)
    backward = lax.cumsum(weighted, axis=1, reverse=True)
    rests = backward[:, 0, :]
    below = entering(rests, n_draw, True, 3)
    suffix = backward + below[:, None, :]
    chained = (
        jnp.power(projected, POWER - 1.0)
        * suffix
        * (1.0 - RMIN)
        * BETA
        * (1.0 - steep * steep)
        / denom
    )
    filtered_sens_t = smooth_each(chained, ids_t, class_radii, n_plan, n_draw, 1)
    filtered_sens = jnp.swapaxes(filtered_sens_t, 1, 2)
    cast_density = jnp.swapaxes(cast_density, 1, 2)
    depth = filtered_sens.shape[2]
    row_count = filtered_sens.shape[0] * filtered_sens.shape[1]
    tiles = lax.axis_size("plan")
    capacity = 4 * row_count // tiles
    row_data = filtered_sens.reshape(row_count, depth)
    patch_ids = row_patch.reshape(row_count)
    owners = patch_ids // PATCH_DEV
    slot_patch = patch_ids - owners * PATCH_DEV
    onehot = (owners[:, None] == jnp.arange(tiles, dtype=jnp.int32)[None, :]).astype(jnp.bfloat16)
    rows = jnp.arange(row_count, dtype=jnp.int32)
    upto = (rows[None, :] <= rows[:, None]).astype(jnp.bfloat16)
    counted = jnp.dot(upto, onehot, preferred_element_type=jnp.float32)
    ranking = jnp.sum(counted * onehot.astype(jnp.float32), axis=1).astype(jnp.int32) - 1
    position = owners * capacity + ranking
    source_row = jnp.full((tiles * capacity,), row_count, jnp.int32).at[position].set(rows)
    table = jnp.concatenate(
        [row_data, jnp.broadcast_to(slot_patch.astype(jnp.float32)[:, None], (row_count, depth))], axis=1)
    table = jnp.concatenate(
        [table, jnp.concatenate([jnp.zeros((1, depth), jnp.float32), jnp.full((1, depth), float(PATCH_DEV))], axis=1)])
    packed = jnp.take(table, source_row, axis=0)
    sendbuf = packed[:, :depth]
    send_ids = packed[:, depth]
    arrived, arrived_ids = (
        lax.all_to_all(
            sendbuf.reshape(tiles, capacity, depth), "plan", split_axis=0, concat_axis=0, tiled=True
        ),
        lax.all_to_all(
            send_ids.reshape(tiles, capacity), "plan", split_axis=0, concat_axis=0, tiled=True
        ),
    )
    picks = (
        jnp.arange(PATCH_DEV, dtype=jnp.int32)[:, None] == arrived_ids.reshape(1, tiles * capacity).astype(jnp.int32)
    ).astype(jnp.float32)
    summed = jnp.dot(picks, arrived.reshape(tiles * capacity, depth), precision=lax.Precision.HIGHEST,
                     preferred_element_type=jnp.float32)
    patch_sens = 0.25 * summed
    return (cast_density, filtered_sens, patch_sens)


def solution(mesh):
    in_specs = (
        P("plan", None, "draw"),
        P("plan", None, "draw"),
        P(),
        P("plan", None, "draw"),
        P("plan", "draw", None),
    )
    out_specs = (P("plan", None, "draw"), P("plan", None, "draw"), P("plan", "draw"))
    return jax.shard_map(
        functools.partial(per_device, mesh.shape["plan"], mesh.shape["draw"]),
        mesh=mesh, in_specs=in_specs, out_specs=out_specs, check_vma=False
    )
```

```python
import functools

import jax
import jax.numpy as jnp
from jax import lax
from jax.experimental import pallas as pl
from jax.experimental.pallas import tpu as pltpu
from jax.sharding import PartitionSpec as P

PATCH_DEV = 512
SWEEPS = 16
HALO = 8

BETA = 8.0
ETA = 0.5
RMIN = 0.2
POWER = 6.0

MESH = pl.DeviceIdType.MESH


def scan_kernel(n_draw, reverse, part_ref, out_ref, held, send_sem, recv_sem):
    p = lax.axis_index("plan")
    d = lax.axis_index("draw")
    held[...] = jnp.zeros_like(held)
    barrier = pltpu.get_barrier_semaphore()
    for e in range(n_draw):
        @pl.when(d != e)
        def _():
            pl.semaphore_signal(barrier, 1, device_id=(p, e), device_id_type=MESH)
    pl.semaphore_wait(barrier, n_draw - 1)

    def later(e):
        return e < d if reverse else e > d

    def earlier(e):
        return e > d if reverse else e < d

    sends = []
    for e in range(n_draw):
        copy = pltpu.make_async_remote_copy(
            part_ref, held.at[d], send_sem.at[e], recv_sem.at[d], device_id=(p, e), device_id_type=MESH)
        sends.append(copy)

        @pl.when(later(e))
        def _():
            copy.start()
    for e in range(n_draw):
        incoming = pltpu.make_async_remote_copy(
            part_ref, held.at[e], send_sem.at[e], recv_sem.at[e], device_id=(p, e), device_id_type=MESH)

        @pl.when(later(e))
        def _():
            sends[e].wait_send()

        @pl.when(earlier(e))
        def _():
            incoming.wait_recv()
    total = held[0]
    for e in range(1, n_draw):
        total = total + held[e]
    out_ref[...] = total


def entering(part, n_draw, reverse, kid):
    vmem = pl.BlockSpec(memory_space=pltpu.VMEM)
    return pl.pallas_call(
        functools.partial(scan_kernel, n_draw, reverse),
        out_shape=jax.ShapeDtypeStruct(part.shape, jnp.float32),
        in_specs=[vmem],
        out_specs=vmem,
        scratch_shapes=[
            pltpu.VMEM((n_draw,) + part.shape, jnp.float32),
            pltpu.SemaphoreType.DMA((n_draw,)),
            pltpu.SemaphoreType.DMA((n_draw,)),
        ],
        compiler_params=pltpu.CompilerParams(collective_id=kid, has_side_effects=True),
    )(part)


def filter_kernel(n_plan, n_draw, src_ref, ids_ref, radii_ref, out_ref, field, cx_ref, cy_ref, cz_ref, inv_ref,
                  send_sem, recv_sem):
    planes, depth, width = src_ref.shape
    for i in range(planes):
        cls = ids_ref[i]
        cx = jnp.zeros((depth, width), jnp.float32)
        cy = jnp.zeros((depth, width), jnp.float32)
        cz = jnp.zeros((depth, width), jnp.float32)
        for level in range(radii_ref.shape[0]):
            hit = cls == level
            cx = jnp.where(hit, radii_ref[level, 0], cx)
            cy = jnp.where(hit, radii_ref[level, 1], cy)
            cz = jnp.where(hit, radii_ref[level, 2], cz)
        cx_ref[i] = cx
        cy_ref[i] = cy
        cz_ref[i] = cz
        inv_ref[i] = 1.0 / (1.0 + 2.0 * (cx + cy + cz))
    p = lax.axis_index("plan")
    d = lax.axis_index("draw")
    has_l = p > 0
    has_r = p < n_plan - 1
    has_b = d > 0
    has_a = d < n_draw - 1
    lo = HALO
    hi = HALO + depth

    field[...] = jnp.zeros_like(field)
    for i in range(planes):
        field[0, i + 1, pl.ds(lo, depth), :] = src_ref[i]

    barrier = pltpu.get_barrier_semaphore()
    neighbours = ((has_l, (p - 1, d)), (has_r, (p + 1, d)), (has_b, (p, d - 1)), (has_a, (p, d + 1)))
    for cond, dev in neighbours:
        @pl.when(cond)
        def _():
            pl.semaphore_signal(barrier, 1, device_id=dev, device_id_type=MESH)
    peers = sum(cond.astype(jnp.int32) for cond, _ in neighbours)
    pl.semaphore_wait(barrier, peers)

    def copies(s):
        to_l = pltpu.make_async_remote_copy(
            field.at[s, 1, pl.ds(lo, depth), :], field.at[s, planes + 1, pl.ds(lo, depth), :],
            send_sem.at[s, 0], recv_sem.at[s, 0], device_id=(p - 1, d), device_id_type=MESH)
        to_r = pltpu.make_async_remote_copy(
            field.at[s, planes, pl.ds(lo, depth), :], field.at[s, 0, pl.ds(lo, depth), :],
            send_sem.at[s, 1], recv_sem.at[s, 1], device_id=(p + 1, d), device_id_type=MESH)
        to_b = pltpu.make_async_remote_copy(
            field.at[s, pl.ds(1, planes), pl.ds(lo, HALO), :], field.at[s, pl.ds(1, planes), pl.ds(hi, HALO), :],
            send_sem.at[s, 2], recv_sem.at[s, 2], device_id=(p, d - 1), device_id_type=MESH)
        to_a = pltpu.make_async_remote_copy(
            field.at[s, pl.ds(1, planes), pl.ds(hi - HALO, HALO), :], field.at[s, pl.ds(1, planes), pl.ds(0, HALO), :],
            send_sem.at[s, 3], recv_sem.at[s, 3], device_id=(p, d + 1), device_id_type=MESH)
        return ((to_l, has_l, has_r), (to_r, has_r, has_l), (to_b, has_b, has_a), (to_a, has_a, has_b))

    def exchange(s):
        group = copies(s)
        for copy, send, _ in group:
            @pl.when(send)
            def _():
                copy.start()
        for copy, send, recv in group:
            @pl.when(send)
            def _():
                copy.wait_send()

            @pl.when(recv)
            def _():
                copy.wait_recv()

    lane = lax.broadcasted_iota(jnp.int32, (depth, width), 1)

    def update(s, i, r0, rows, last):
        at = lo + r0
        c = field[s, i + 1, pl.ds(at, rows), :]
        zm = field[s, i + 1, pl.ds(at - 1, rows), :]
        zp = field[s, i + 1, pl.ds(at + 1, rows), :]
        xm = field[s, i, pl.ds(at, rows), :]
        xp = field[s, i + 2, pl.ds(at, rows), :]
        lanes = lane[:rows]
        ym = jnp.where(lanes == 0, 0.0, pltpu.roll(c, 1, 1))
        yp = jnp.where(lanes == width - 1, 0.0, pltpu.roll(c, width - 1, 1))
        part = pl.ds(r0, rows)
        new = (src_ref[i, part, :] + cx_ref[i, part, :] * (xm + xp) + cy_ref[i, part, :] * (ym + yp)
               + cz_ref[i, part, :] * (zm + zp)) * inv_ref[i, part, :]
        if last:
            out_ref[i, part, :] = new
        else:
            field[1 - s, i + 1, pl.ds(at, rows), :] = new

    def sweep_send(s):
        t = 1 - s
        group = copies(t)
        update(s, 0, 0, depth, False)
        update(s, planes - 1, 0, depth, False)
        for copy, send, _ in group[:2]:
            @pl.when(send)
            def _():
                copy.start()
        for i in range(1, planes - 1):
            update(s, i, 0, HALO, False)
            update(s, i, depth - HALO, HALO, False)
        for copy, send, _ in group[2:]:
            @pl.when(send)
            def _():
                copy.start()
        for i in range(1, planes - 1):
            update(s, i, HALO, depth - 2 * HALO, False)
        for copy, send, recv in group:
            @pl.when(send)
            def _():
                copy.wait_send()

            @pl.when(recv)
            def _():
                copy.wait_recv()

    exchange(0)

    def pair(k, carry):
        sweep_send(0)
        sweep_send(1)
        return carry

    lax.fori_loop(0, SWEEPS // 2 - 1, pair, 0)
    sweep_send(0)
    for i in range(planes):
        update(1, i, 0, depth, True)


def smooth_each(source, class_ids, class_radii, n_plan, n_draw, kid):
    planes, depth, width = source.shape
    vmem = pl.BlockSpec(memory_space=pltpu.VMEM)
    smem = pl.BlockSpec(memory_space=pltpu.SMEM)
    return pl.pallas_call(
        functools.partial(filter_kernel, n_plan, n_draw),
        out_shape=jax.ShapeDtypeStruct(source.shape, jnp.float32),
        in_specs=[vmem, vmem, smem],
        out_specs=vmem,
        scratch_shapes=[
            pltpu.VMEM((2, planes + 2, depth + 2 * HALO, width), jnp.float32),
            pltpu.VMEM(source.shape, jnp.float32),
            pltpu.VMEM(source.shape, jnp.float32),
            pltpu.VMEM(source.shape, jnp.float32),
            pltpu.VMEM(source.shape, jnp.float32),
            pltpu.SemaphoreType.DMA((2, 4)),
            pltpu.SemaphoreType.DMA((2, 4)),
        ],
        compiler_params=pltpu.CompilerParams(collective_id=kid, has_side_effects=True),
    )(source, class_ids, class_radii)


def per_device(n_plan, n_draw, design, class_ids, class_radii, sensitivity, row_patch):
    design_t = jnp.swapaxes(design, 1, 2)
    ids_t = jnp.swapaxes(class_ids, 1, 2)
    sens_t = jnp.swapaxes(sensitivity, 1, 2)
    filtered = smooth_each(design_t, ids_t, class_radii, n_plan, n_draw, 0)
    denom = jnp.tanh(jnp.float32(BETA * ETA)) + jnp.tanh(jnp.float32(BETA * (1.0 - ETA)))
    steep = jnp.tanh(BETA * (filtered - ETA))
    projected = RMIN + (1.0 - RMIN) * (jnp.tanh(jnp.float32(BETA * ETA)) + steep) / denom
    running = jnp.cumsum(jnp.power(projected, POWER), axis=1)
    totals = running[:, -1, :]
    carried = entering(totals, n_draw, False, 2)
    prefix = running + carried[:, None, :]
    cast_density = jnp.power(prefix, 1.0 / POWER)
    weighted = sens_t * jnp.power(prefix, (1.0 - POWER) / POWER)
    backward = lax.cumsum(weighted, axis=1, reverse=True)
    rests = backward[:, 0, :]
    below = entering(rests, n_draw, True, 3)
    suffix = backward + below[:, None, :]
    chained = (
        jnp.power(projected, POWER - 1.0)
        * suffix
        * (1.0 - RMIN)
        * BETA
        * (1.0 - steep * steep)
        / denom
    )
    filtered_sens_t = smooth_each(chained, ids_t, class_radii, n_plan, n_draw, 1)
    filtered_sens = jnp.swapaxes(filtered_sens_t, 1, 2)
    cast_density = jnp.swapaxes(cast_density, 1, 2)
    depth = filtered_sens.shape[2]
    row_count = filtered_sens.shape[0] * filtered_sens.shape[1]
    tiles = lax.axis_size("plan")
    capacity = 4 * row_count // tiles
    row_data = filtered_sens.reshape(row_count, depth)
    patch_ids = row_patch.reshape(row_count)
    owners = patch_ids // PATCH_DEV
    slot_patch = patch_ids - owners * PATCH_DEV
    onehot = (owners[:, None] == jnp.arange(tiles, dtype=jnp.int32)[None, :]).astype(jnp.bfloat16)
    rows = jnp.arange(row_count, dtype=jnp.int32)
    upto = (rows[None, :] <= rows[:, None]).astype(jnp.bfloat16)
    counted = jnp.dot(upto, onehot, preferred_element_type=jnp.float32)
    ranking = jnp.sum(counted * onehot.astype(jnp.float32), axis=1).astype(jnp.int32) - 1
    position = owners * capacity + ranking
    source_row = jnp.full((tiles * capacity,), row_count, jnp.int32).at[position].set(rows)
    table = jnp.concatenate(
        [row_data, jnp.broadcast_to(slot_patch.astype(jnp.float32)[:, None], (row_count, depth))], axis=1)
    table = jnp.concatenate(
        [table, jnp.concatenate([jnp.zeros((1, depth), jnp.float32), jnp.full((1, depth), float(PATCH_DEV))], axis=1)])
    packed = jnp.take(table, source_row, axis=0)
    id_rows = capacity // depth
    sendbuf = jnp.concatenate(
        [
            packed[:, :depth].reshape(tiles, capacity, depth),
            packed[:, depth].reshape(tiles, id_rows, depth),
            jnp.zeros((tiles, (-id_rows) % 8, depth), jnp.float32),
        ],
        axis=1,
    )
    arrived_all = lax.all_to_all(sendbuf, "plan", split_axis=0, concat_axis=0, tiled=True)
    arrived = arrived_all[:, :capacity, :]
    arrived_ids = arrived_all[:, capacity:capacity + id_rows, :]
    picks = (
        jnp.arange(PATCH_DEV, dtype=jnp.int32)[:, None] == arrived_ids.reshape(1, tiles * capacity).astype(jnp.int32)
    ).astype(jnp.float32)
    summed = jnp.dot(picks, arrived.reshape(tiles * capacity, depth), precision=lax.Precision.HIGHEST,
                     preferred_element_type=jnp.float32)
    patch_sens = 0.25 * summed
    return (cast_density, filtered_sens, patch_sens)


def solution(mesh):
    in_specs = (
        P("plan", None, "draw"),
        P("plan", None, "draw"),
        P(),
        P("plan", None, "draw"),
        P("plan", "draw", None),
    )
    out_specs = (P("plan", None, "draw"), P("plan", None, "draw"), P("plan", "draw"))
    return jax.shard_map(
        functools.partial(per_device, mesh.shape["plan"], mesh.shape["draw"]),
        mesh=mesh, in_specs=in_specs, out_specs=out_specs, check_vma=False
    )
```

```python
import functools

import jax
import jax.numpy as jnp
from jax import lax
from jax.experimental import pallas as pl
from jax.experimental.pallas import tpu as pltpu
from jax.sharding import PartitionSpec as P

PATCH_DEV = 512
SWEEPS = 16
HALO = 8

BETA = 8.0
ETA = 0.5
RMIN = 0.2
POWER = 6.0

MESH = pl.DeviceIdType.MESH


def scan_kernel(n_draw, reverse, part_ref, out_ref, held, send_sem, recv_sem):
    p = lax.axis_index("plan")
    d = lax.axis_index("draw")
    held[...] = jnp.zeros_like(held)
    barrier = pltpu.get_barrier_semaphore()
    for e in range(n_draw):
        @pl.when(d != e)
        def _():
            pl.semaphore_signal(barrier, 1, device_id=(p, e), device_id_type=MESH)
    pl.semaphore_wait(barrier, n_draw - 1)

    def later(e):
        return e < d if reverse else e > d

    def earlier(e):
        return e > d if reverse else e < d

    sends = []
    for e in range(n_draw):
        copy = pltpu.make_async_remote_copy(
            part_ref, held.at[d], send_sem.at[e], recv_sem.at[d], device_id=(p, e), device_id_type=MESH)
        sends.append(copy)

        @pl.when(later(e))
        def _():
            copy.start()
    for e in range(n_draw):
        incoming = pltpu.make_async_remote_copy(
            part_ref, held.at[e], send_sem.at[e], recv_sem.at[e], device_id=(p, e), device_id_type=MESH)

        @pl.when(later(e))
        def _():
            sends[e].wait_send()

        @pl.when(earlier(e))
        def _():
            incoming.wait_recv()
    total = held[0]
    for e in range(1, n_draw):
        total = total + held[e]
    out_ref[...] = total


def entering(part, n_draw, reverse, kid):
    vmem = pl.BlockSpec(memory_space=pltpu.VMEM)
    return pl.pallas_call(
        functools.partial(scan_kernel, n_draw, reverse),
        out_shape=jax.ShapeDtypeStruct(part.shape, jnp.float32),
        in_specs=[vmem],
        out_specs=vmem,
        scratch_shapes=[
            pltpu.VMEM((n_draw,) + part.shape, jnp.float32),
            pltpu.SemaphoreType.DMA((n_draw,)),
            pltpu.SemaphoreType.DMA((n_draw,)),
        ],
        compiler_params=pltpu.CompilerParams(collective_id=kid, has_side_effects=True),
    )(part)


WIDE = 2
DIRS = ((-1, 0), (1, 0), (0, -1), (0, 1), (-1, -1), (-1, 1), (1, -1), (1, 1))


def opposite(k):
    dp, dd = DIRS[k]
    return DIRS.index((-dp, -dd))


def filter_kernel(n_plan, n_draw, src_ref, ids_ref, radii_ref, out_ref, field, src_e, ids_e, cx_e, cy_e, cz_e,
                  inv_e, init_send, init_recv, send_sem, recv_sem, credit):
    planes, depth, width = src_ref.shape
    ext_planes = planes + 2 * WIDE
    rows = depth + 2 * HALO
    p = lax.axis_index("plan")
    d = lax.axis_index("draw")

    def exists(k):
        dp, dd = DIRS[k]
        ok_p = (p + dp >= 0) & (p + dp < n_plan)
        ok_d = (d + dd >= 0) & (d + dd < n_draw)
        if dp and dd:
            return ok_p & ok_d
        return ok_p if dp else ok_d

    def regions(k):
        dp, dd = DIRS[k]
        if dp < 0:
            src_p, dst_p = pl.ds(WIDE, WIDE), pl.ds(WIDE + planes, WIDE)
        elif dp > 0:
            src_p, dst_p = pl.ds(planes, WIDE), pl.ds(0, WIDE)
        else:
            src_p, dst_p = pl.ds(WIDE, planes), pl.ds(WIDE, planes)
        if dd < 0:
            src_r, dst_r = pl.ds(HALO, HALO), pl.ds(HALO + depth, HALO)
        elif dd > 0:
            src_r, dst_r = pl.ds(depth, HALO), pl.ds(0, HALO)
        else:
            src_r, dst_r = pl.ds(HALO, depth), pl.ds(HALO, depth)
        return src_p, src_r, dst_p, dst_r

    def target(k):
        dp, dd = DIRS[k]
        return (p + dp, d + dd)

    field[...] = jnp.zeros_like(field)
    src_e[...] = jnp.zeros_like(src_e)
    ids_e[...] = jnp.zeros_like(ids_e)
    for i in range(planes):
        src_e[WIDE + i, pl.ds(HALO, depth), :] = src_ref[i]
        ids_e[WIDE + i, pl.ds(HALO, depth), :] = ids_ref[i]

    barrier = pltpu.get_barrier_semaphore()
    for k in range(len(DIRS)):
        @pl.when(exists(k))
        def _():
            pl.semaphore_signal(barrier, 1, device_id=target(k), device_id_type=MESH)
    peers = sum(exists(k).astype(jnp.int32) for k in range(len(DIRS)))
    pl.semaphore_wait(barrier, peers)

    def run(copies):
        for copy, k in copies:
            @pl.when(exists(k))
            def _():
                copy.start()
        for copy, k in copies:
            @pl.when(exists(k))
            def _():
                copy.wait_send()

            @pl.when(exists(opposite(k)))
            def _():
                copy.wait_recv()

    init = []
    for which, buf in enumerate((src_e, ids_e)):
        for k in range(len(DIRS)):
            sp, sr, dp_, dr = regions(k)
            init.append((pltpu.make_async_remote_copy(
                buf.at[sp, sr, :], buf.at[dp_, dr, :], init_send.at[which, k], init_recv.at[which, k],
                device_id=target(k), device_id_type=MESH), k))
    run(init)

    row_id = lax.broadcasted_iota(jnp.int32, (rows, width), 0)
    for i in range(ext_planes):
        cls = ids_e[i]
        cx = jnp.zeros((rows, width), jnp.float32)
        cy = jnp.zeros((rows, width), jnp.float32)
        cz = jnp.zeros((rows, width), jnp.float32)
        for level in range(radii_ref.shape[0]):
            hit = cls == level
            cx = jnp.where(hit, radii_ref[level, 0], cx)
            cy = jnp.where(hit, radii_ref[level, 1], cy)
            cz = jnp.where(hit, radii_ref[level, 2], cz)
        cx_e[i] = cx
        cy_e[i] = cy
        cz_e[i] = cz
        outside = (row_id < HALO) & (d == 0)
        outside = outside | ((row_id >= HALO + depth) & (d == n_draw - 1))
        if i < WIDE:
            outside = outside | (p == 0)
        if i >= WIDE + planes:
            outside = outside | (p == n_plan - 1)
        inv_e[i] = jnp.where(outside, 0.0, 1.0 / (1.0 + 2.0 * (cx + cy + cz)))
        field[0, i] = src_e[i]

    lane = lax.broadcasted_iota(jnp.int32, (rows, width), 1)

    def wide_update(s, i):
        c = field[s, i]
        zm = pltpu.roll(c, 1, 0)
        zp = pltpu.roll(c, rows - 1, 0)
        ym = jnp.where(lane == 0, 0.0, pltpu.roll(c, 1, 1))
        yp = jnp.where(lane == width - 1, 0.0, pltpu.roll(c, width - 1, 1))
        new = (src_e[i] + cx_e[i] * (field[s, i - 1] + field[s, i + 1]) + cy_e[i] * (ym + yp)
               + cz_e[i] * (zm + zp)) * inv_e[i]
        field[1 - s, i] = new

    def core_update(s, i, last):
        part = pl.ds(HALO, depth)
        c = field[s, i, part, :]
        zm = field[s, i, pl.ds(HALO - 1, depth), :]
        zp = field[s, i, pl.ds(HALO + 1, depth), :]
        lanes = lane[:depth]
        ym = jnp.where(lanes == 0, 0.0, pltpu.roll(c, 1, 1))
        yp = jnp.where(lanes == width - 1, 0.0, pltpu.roll(c, width - 1, 1))
        new = (src_e[i, part, :] + cx_e[i, part, :] * (field[s, i - 1, part, :] + field[s, i + 1, part, :])
               + cy_e[i, part, :] * (ym + yp) + cz_e[i, part, :] * (zm + zp)) * inv_e[i, part, :]
        if last:
            out_ref[i - WIDE] = new
        else:
            field[1 - s, i, part, :] = new

    def group(first, last):
        if not first:
            copies = []
            for k in range(len(DIRS)):
                sp, sr, dp_, dr = regions(k)

                @pl.when(exists(k))
                def _():
                    pl.semaphore_wait(credit.at[opposite(k)], 1)
                copies.append((pltpu.make_async_remote_copy(
                    field.at[0, sp, sr, :], field.at[0, dp_, dr, :], send_sem.at[k], recv_sem.at[k],
                    device_id=target(k), device_id_type=MESH), k))
            run(copies)
        for j in range(WIDE):
            s = j % 2
            e = WIDE - 1 - j
            if e > 0:
                for i in range(WIDE - e, WIDE + planes + e):
                    wide_update(s, i)
            else:
                for i in range(WIDE, WIDE + planes):
                    core_update(s, i, last)
            if j == 0 and not last:
                for k in range(len(DIRS)):
                    @pl.when(exists(k))
                    def _():
                        pl.semaphore_signal(credit.at[k], 1, device_id=target(k), device_id_type=MESH)

    group(True, False)

    def middle(g, carry):
        group(False, False)
        return carry

    lax.fori_loop(0, SWEEPS // WIDE - 2, middle, 0)
    group(False, True)


def smooth_each(source, class_ids, class_radii, n_plan, n_draw, kid):
    planes, depth, width = source.shape
    vmem = pl.BlockSpec(memory_space=pltpu.VMEM)
    smem = pl.BlockSpec(memory_space=pltpu.SMEM)
    return pl.pallas_call(
        functools.partial(filter_kernel, n_plan, n_draw),
        out_shape=jax.ShapeDtypeStruct(source.shape, jnp.float32),
        in_specs=[vmem, vmem, smem],
        out_specs=vmem,
        scratch_shapes=[
            pltpu.VMEM((2, planes + 2 * WIDE, depth + 2 * HALO, width), jnp.float32),
            pltpu.VMEM((planes + 2 * WIDE, depth + 2 * HALO, width), jnp.float32),
            pltpu.VMEM((planes + 2 * WIDE, depth + 2 * HALO, width), jnp.int32),
            pltpu.VMEM((planes + 2 * WIDE, depth + 2 * HALO, width), jnp.float32),
            pltpu.VMEM((planes + 2 * WIDE, depth + 2 * HALO, width), jnp.float32),
            pltpu.VMEM((planes + 2 * WIDE, depth + 2 * HALO, width), jnp.float32),
            pltpu.VMEM((planes + 2 * WIDE, depth + 2 * HALO, width), jnp.float32),
            pltpu.SemaphoreType.DMA((2, len(DIRS))),
            pltpu.SemaphoreType.DMA((2, len(DIRS))),
            pltpu.SemaphoreType.DMA((len(DIRS),)),
            pltpu.SemaphoreType.DMA((len(DIRS),)),
            pltpu.SemaphoreType.REGULAR((len(DIRS),)),
        ],
        compiler_params=pltpu.CompilerParams(collective_id=kid, has_side_effects=True),
    )(source, class_ids, class_radii)


def per_device(n_plan, n_draw, design, class_ids, class_radii, sensitivity, row_patch):
    design_t = jnp.swapaxes(design, 1, 2)
    ids_t = jnp.swapaxes(class_ids, 1, 2)
    sens_t = jnp.swapaxes(sensitivity, 1, 2)
    filtered = smooth_each(design_t, ids_t, class_radii, n_plan, n_draw, 0)
    denom = jnp.tanh(jnp.float32(BETA * ETA)) + jnp.tanh(jnp.float32(BETA * (1.0 - ETA)))
    steep = jnp.tanh(BETA * (filtered - ETA))
    projected = RMIN + (1.0 - RMIN) * (jnp.tanh(jnp.float32(BETA * ETA)) + steep) / denom
    running = jnp.cumsum(jnp.power(projected, POWER), axis=1)
    totals = running[:, -1, :]
    carried = entering(totals, n_draw, False, 2)
    prefix = running + carried[:, None, :]
    cast_density = jnp.power(prefix, 1.0 / POWER)
    weighted = sens_t * jnp.power(prefix, (1.0 - POWER) / POWER)
    backward = lax.cumsum(weighted, axis=1, reverse=True)
    rests = backward[:, 0, :]
    below = entering(rests, n_draw, True, 3)
    suffix = backward + below[:, None, :]
    chained = (
        jnp.power(projected, POWER - 1.0)
        * suffix
        * (1.0 - RMIN)
        * BETA
        * (1.0 - steep * steep)
        / denom
    )
    filtered_sens_t = smooth_each(chained, ids_t, class_radii, n_plan, n_draw, 1)
    filtered_sens = jnp.swapaxes(filtered_sens_t, 1, 2)
    cast_density = jnp.swapaxes(cast_density, 1, 2)
    depth = filtered_sens.shape[2]
    row_count = filtered_sens.shape[0] * filtered_sens.shape[1]
    tiles = lax.axis_size("plan")
    capacity = 4 * row_count // tiles
    row_data = filtered_sens.reshape(row_count, depth)
    patch_ids = row_patch.reshape(row_count)
    owners = patch_ids // PATCH_DEV
    slot_patch = patch_ids - owners * PATCH_DEV
    onehot = (owners[:, None] == jnp.arange(tiles, dtype=jnp.int32)[None, :]).astype(jnp.bfloat16)
    rows = jnp.arange(row_count, dtype=jnp.int32)
    upto = (rows[None, :] <= rows[:, None]).astype(jnp.bfloat16)
    counted = jnp.dot(upto, onehot, preferred_element_type=jnp.float32)
    ranking = jnp.sum(counted * onehot.astype(jnp.float32), axis=1).astype(jnp.int32) - 1
    position = owners * capacity + ranking
    source_row = jnp.full((tiles * capacity,), row_count, jnp.int32).at[position].set(rows)
    table = jnp.concatenate(
        [row_data, jnp.broadcast_to(slot_patch.astype(jnp.float32)[:, None], (row_count, depth))], axis=1)
    table = jnp.concatenate(
        [table, jnp.concatenate([jnp.zeros((1, depth), jnp.float32), jnp.full((1, depth), float(PATCH_DEV))], axis=1)])
    packed = jnp.take(table, source_row, axis=0)
    id_rows = capacity // depth
    sendbuf = jnp.concatenate(
        [
            packed[:, :depth].reshape(tiles, capacity, depth),
            packed[:, depth].reshape(tiles, id_rows, depth),
            jnp.zeros((tiles, (-id_rows) % 8, depth), jnp.float32),
        ],
        axis=1,
    )
    arrived_all = lax.all_to_all(sendbuf, "plan", split_axis=0, concat_axis=0, tiled=True)
    arrived = arrived_all[:, :capacity, :]
    arrived_ids = arrived_all[:, capacity:capacity + id_rows, :]
    picks = (
        jnp.arange(PATCH_DEV, dtype=jnp.int32)[:, None] == arrived_ids.reshape(1, tiles * capacity).astype(jnp.int32)
    ).astype(jnp.float32)
    summed = jnp.dot(picks, arrived.reshape(tiles * capacity, depth), precision=lax.Precision.HIGHEST,
                     preferred_element_type=jnp.float32)
    patch_sens = 0.25 * summed
    return (cast_density, filtered_sens, patch_sens)


def solution(mesh):
    in_specs = (
        P("plan", None, "draw"),
        P("plan", None, "draw"),
        P(),
        P("plan", None, "draw"),
        P("plan", "draw", None),
    )
    out_specs = (P("plan", None, "draw"), P("plan", None, "draw"), P("plan", "draw"))
    return jax.shard_map(
        functools.partial(per_device, mesh.shape["plan"], mesh.shape["draw"]),
        mesh=mesh, in_specs=in_specs, out_specs=out_specs, check_vma=False
    )
```

```python
import functools

import jax
import jax.numpy as jnp
from jax import lax
from jax.experimental import pallas as pl
from jax.experimental.pallas import tpu as pltpu
from jax.sharding import PartitionSpec as P

PATCH_DEV = 512
SWEEPS = 16
HALO = 8

BETA = 8.0
ETA = 0.5
RMIN = 0.2
POWER = 6.0

MESH = pl.DeviceIdType.MESH


def scan_kernel(n_draw, reverse, part_ref, out_ref, held, send_sem, recv_sem):
    p = lax.axis_index("plan")
    d = lax.axis_index("draw")
    held[...] = jnp.zeros_like(held)
    barrier = pltpu.get_barrier_semaphore()
    for e in range(n_draw):
        @pl.when(d != e)
        def _():
            pl.semaphore_signal(barrier, 1, device_id=(p, e), device_id_type=MESH)
    pl.semaphore_wait(barrier, n_draw - 1)

    def later(e):
        return e < d if reverse else e > d

    def earlier(e):
        return e > d if reverse else e < d

    sends = []
    for e in range(n_draw):
        copy = pltpu.make_async_remote_copy(
            part_ref, held.at[d], send_sem.at[e], recv_sem.at[d], device_id=(p, e), device_id_type=MESH)
        sends.append(copy)

        @pl.when(later(e))
        def _():
            copy.start()
    for e in range(n_draw):
        incoming = pltpu.make_async_remote_copy(
            part_ref, held.at[e], send_sem.at[e], recv_sem.at[e], device_id=(p, e), device_id_type=MESH)

        @pl.when(later(e))
        def _():
            sends[e].wait_send()

        @pl.when(earlier(e))
        def _():
            incoming.wait_recv()
    total = held[0]
    for e in range(1, n_draw):
        total = total + held[e]
    out_ref[...] = total


def entering(part, n_draw, reverse, kid):
    vmem = pl.BlockSpec(memory_space=pltpu.VMEM)
    return pl.pallas_call(
        functools.partial(scan_kernel, n_draw, reverse),
        out_shape=jax.ShapeDtypeStruct(part.shape, jnp.float32),
        in_specs=[vmem],
        out_specs=vmem,
        scratch_shapes=[
            pltpu.VMEM((n_draw,) + part.shape, jnp.float32),
            pltpu.SemaphoreType.DMA((n_draw,)),
            pltpu.SemaphoreType.DMA((n_draw,)),
        ],
        compiler_params=pltpu.CompilerParams(collective_id=kid, has_side_effects=True),
    )(part)


def filter_kernel(n_plan, n_draw, src_ref, ids_ref, radii_ref, out_ref, field, cx_ref, cy_ref, cz_ref, inv_ref,
                  send_sem, recv_sem):
    planes, depth, width = src_ref.shape
    for i in range(planes):
        cls = ids_ref[i]
        cx = jnp.zeros((depth, width), jnp.float32)
        cy = jnp.zeros((depth, width), jnp.float32)
        cz = jnp.zeros((depth, width), jnp.float32)
        for level in range(radii_ref.shape[0]):
            hit = cls == level
            cx = jnp.where(hit, radii_ref[level, 0], cx)
            cy = jnp.where(hit, radii_ref[level, 1], cy)
            cz = jnp.where(hit, radii_ref[level, 2], cz)
        cx_ref[i] = cx
        cy_ref[i] = cy
        cz_ref[i] = cz
        inv_ref[i] = 1.0 / (1.0 + 2.0 * (cx + cy + cz))
    p = lax.axis_index("plan")
    d = lax.axis_index("draw")
    has_l = p > 0
    has_r = p < n_plan - 1
    has_b = d > 0
    has_a = d < n_draw - 1
    lo = HALO
    hi = HALO + depth

    field[...] = jnp.zeros_like(field)
    for i in range(planes):
        field[0, i + 1, pl.ds(lo, depth), :] = src_ref[i]

    barrier = pltpu.get_barrier_semaphore()
    neighbours = ((has_l, (p - 1, d)), (has_r, (p + 1, d)), (has_b, (p, d - 1)), (has_a, (p, d + 1)))
    for cond, dev in neighbours:
        @pl.when(cond)
        def _():
            pl.semaphore_signal(barrier, 1, device_id=dev, device_id_type=MESH)
    peers = sum(cond.astype(jnp.int32) for cond, _ in neighbours)
    pl.semaphore_wait(barrier, peers)

    def copies(s):
        to_l = pltpu.make_async_remote_copy(
            field.at[s, 1, pl.ds(lo, depth), :], field.at[s, planes + 1, pl.ds(lo, depth), :],
            send_sem.at[s, 0], recv_sem.at[s, 0], device_id=(p - 1, d), device_id_type=MESH)
        to_r = pltpu.make_async_remote_copy(
            field.at[s, planes, pl.ds(lo, depth), :], field.at[s, 0, pl.ds(lo, depth), :],
            send_sem.at[s, 1], recv_sem.at[s, 1], device_id=(p + 1, d), device_id_type=MESH)
        to_b = pltpu.make_async_remote_copy(
            field.at[s, pl.ds(1, planes), pl.ds(lo, HALO), :], field.at[s, pl.ds(1, planes), pl.ds(hi, HALO), :],
            send_sem.at[s, 2], recv_sem.at[s, 2], device_id=(p, d - 1), device_id_type=MESH)
        to_a = pltpu.make_async_remote_copy(
            field.at[s, pl.ds(1, planes), pl.ds(hi - HALO, HALO), :], field.at[s, pl.ds(1, planes), pl.ds(0, HALO), :],
            send_sem.at[s, 3], recv_sem.at[s, 3], device_id=(p, d + 1), device_id_type=MESH)
        return ((to_l, has_l, has_r), (to_r, has_r, has_l), (to_b, has_b, has_a), (to_a, has_a, has_b))

    def exchange(s):
        group = copies(s)
        for copy, send, _ in group:
            @pl.when(send)
            def _():
                copy.start()
        for copy, send, recv in group:
            @pl.when(send)
            def _():
                copy.wait_send()

            @pl.when(recv)
            def _():
                copy.wait_recv()

    lane = lax.broadcasted_iota(jnp.int32, (depth, width), 1)

    def update(s, i, r0, rows, last):
        at = lo + r0
        c = field[s, i + 1, pl.ds(at, rows), :]
        zm = field[s, i + 1, pl.ds(at - 1, rows), :]
        zp = field[s, i + 1, pl.ds(at + 1, rows), :]
        xm = field[s, i, pl.ds(at, rows), :]
        xp = field[s, i + 2, pl.ds(at, rows), :]
        lanes = lane[:rows]
        ym = jnp.where(lanes == 0, 0.0, pltpu.roll(c, 1, 1))
        yp = jnp.where(lanes == width - 1, 0.0, pltpu.roll(c, width - 1, 1))
        part = pl.ds(r0, rows)
        new = (src_ref[i, part, :] + cx_ref[i, part, :] * (xm + xp) + cy_ref[i, part, :] * (ym + yp)
               + cz_ref[i, part, :] * (zm + zp)) * inv_ref[i, part, :]
        if last:
            out_ref[i, part, :] = new
        else:
            field[1 - s, i + 1, pl.ds(at, rows), :] = new

    def sweep_send(s):
        t = 1 - s
        group = copies(t)
        update(s, 0, 0, depth, False)
        update(s, planes - 1, 0, depth, False)
        for copy, send, _ in group[:2]:
            @pl.when(send)
            def _():
                copy.start()
        for i in range(1, planes - 1):
            update(s, i, 0, HALO, False)
            update(s, i, depth - HALO, HALO, False)
        for copy, send, _ in group[2:]:
            @pl.when(send)
            def _():
                copy.start()
        for i in range(1, planes - 1):
            update(s, i, HALO, depth - 2 * HALO, False)
        for copy, send, recv in group:
            @pl.when(send)
            def _():
                copy.wait_send()

            @pl.when(recv)
            def _():
                copy.wait_recv()

    exchange(0)

    def pair(k, carry):
        sweep_send(0)
        sweep_send(1)
        return carry

    lax.fori_loop(0, SWEEPS // 2 - 1, pair, 0)
    sweep_send(0)
    for i in range(planes):
        update(1, i, 0, depth, True)


def exchange_kernel(n_plan, send_ref, out_ref, send_sem, recv_sem, local_sem):
    p = lax.axis_index("plan")
    d = lax.axis_index("draw")
    barrier = pltpu.get_barrier_semaphore()
    for e in range(n_plan):
        @pl.when(e != p)
        def _():
            pl.semaphore_signal(barrier, 1, device_id=(e, d), device_id_type=MESH)
    pl.semaphore_wait(barrier, n_plan - 1)
    local = pltpu.make_async_copy(send_ref.at[p], out_ref.at[p], local_sem)
    local.start()
    sends = []
    for e in range(n_plan):
        copy = pltpu.make_async_remote_copy(
            send_ref.at[e], out_ref.at[p], send_sem.at[e], recv_sem.at[p], device_id=(e, d), device_id_type=MESH)
        sends.append(copy)

        @pl.when(e != p)
        def _():
            copy.start()
    for e in range(n_plan):
        incoming = pltpu.make_async_remote_copy(
            send_ref.at[e], out_ref.at[e], send_sem.at[e], recv_sem.at[e], device_id=(e, d), device_id_type=MESH)

        @pl.when(e != p)
        def _():
            sends[e].wait_send()
            incoming.wait_recv()
    local.wait()


def exchange_rows(sendbuf, n_plan, kid):
    vmem = pl.BlockSpec(memory_space=pltpu.VMEM)
    return pl.pallas_call(
        functools.partial(exchange_kernel, n_plan),
        out_shape=jax.ShapeDtypeStruct(sendbuf.shape, jnp.float32),
        in_specs=[vmem],
        out_specs=vmem,
        scratch_shapes=[
            pltpu.SemaphoreType.DMA((n_plan,)),
            pltpu.SemaphoreType.DMA((n_plan,)),
            pltpu.SemaphoreType.DMA(()),
        ],
        compiler_params=pltpu.CompilerParams(collective_id=kid, has_side_effects=True),
    )(sendbuf)


def smooth_each(source, class_ids, class_radii, n_plan, n_draw, kid):
    planes, depth, width = source.shape
    vmem = pl.BlockSpec(memory_space=pltpu.VMEM)
    smem = pl.BlockSpec(memory_space=pltpu.SMEM)
    return pl.pallas_call(
        functools.partial(filter_kernel, n_plan, n_draw),
        out_shape=jax.ShapeDtypeStruct(source.shape, jnp.float32),
        in_specs=[vmem, vmem, smem],
        out_specs=vmem,
        scratch_shapes=[
            pltpu.VMEM((2, planes + 2, depth + 2 * HALO, width), jnp.float32),
            pltpu.VMEM(source.shape, jnp.float32),
            pltpu.VMEM(source.shape, jnp.float32),
            pltpu.VMEM(source.shape, jnp.float32),
            pltpu.VMEM(source.shape, jnp.float32),
            pltpu.SemaphoreType.DMA((2, 4)),
            pltpu.SemaphoreType.DMA((2, 4)),
        ],
        compiler_params=pltpu.CompilerParams(collective_id=kid, has_side_effects=True),
    )(source, class_ids, class_radii)


def per_device(n_plan, n_draw, design, class_ids, class_radii, sensitivity, row_patch):
    design_t = jnp.swapaxes(design, 1, 2)
    ids_t = jnp.swapaxes(class_ids, 1, 2)
    sens_t = jnp.swapaxes(sensitivity, 1, 2)
    filtered = smooth_each(design_t, ids_t, class_radii, n_plan, n_draw, 0)
    denom = jnp.tanh(jnp.float32(BETA * ETA)) + jnp.tanh(jnp.float32(BETA * (1.0 - ETA)))
    steep = jnp.tanh(BETA * (filtered - ETA))
    projected = RMIN + (1.0 - RMIN) * (jnp.tanh(jnp.float32(BETA * ETA)) + steep) / denom
    running = jnp.cumsum(jnp.power(projected, POWER), axis=1)
    totals = running[:, -1, :]
    carried = entering(totals, n_draw, False, 2)
    prefix = running + carried[:, None, :]
    cast_density = jnp.power(prefix, 1.0 / POWER)
    weighted = sens_t * jnp.power(prefix, (1.0 - POWER) / POWER)
    backward = lax.cumsum(weighted, axis=1, reverse=True)
    rests = backward[:, 0, :]
    below = entering(rests, n_draw, True, 3)
    suffix = backward + below[:, None, :]
    chained = (
        jnp.power(projected, POWER - 1.0)
        * suffix
        * (1.0 - RMIN)
        * BETA
        * (1.0 - steep * steep)
        / denom
    )
    filtered_sens_t = smooth_each(chained, ids_t, class_radii, n_plan, n_draw, 1)
    filtered_sens = jnp.swapaxes(filtered_sens_t, 1, 2)
    cast_density = jnp.swapaxes(cast_density, 1, 2)
    depth = filtered_sens.shape[2]
    row_count = filtered_sens.shape[0] * filtered_sens.shape[1]
    tiles = lax.axis_size("plan")
    capacity = 4 * row_count // tiles
    row_data = filtered_sens.reshape(row_count, depth)
    patch_ids = row_patch.reshape(row_count)
    owners = patch_ids // PATCH_DEV
    slot_patch = patch_ids - owners * PATCH_DEV
    onehot = (owners[:, None] == jnp.arange(tiles, dtype=jnp.int32)[None, :]).astype(jnp.bfloat16)
    rows = jnp.arange(row_count, dtype=jnp.int32)
    upto = (rows[None, :] <= rows[:, None]).astype(jnp.bfloat16)
    counted = jnp.dot(upto, onehot, preferred_element_type=jnp.float32)
    ranking = jnp.sum(counted * onehot.astype(jnp.float32), axis=1).astype(jnp.int32) - 1
    position = owners * capacity + ranking
    source_row = jnp.full((tiles * capacity,), row_count, jnp.int32).at[position].set(rows)
    table = jnp.concatenate(
        [row_data, jnp.broadcast_to(slot_patch.astype(jnp.float32)[:, None], (row_count, depth))], axis=1)
    table = jnp.concatenate(
        [table, jnp.concatenate([jnp.zeros((1, depth), jnp.float32), jnp.full((1, depth), float(PATCH_DEV))], axis=1)])
    packed = jnp.take(table, source_row, axis=0)
    id_rows = capacity // depth
    sendbuf = jnp.concatenate(
        [
            packed[:, :depth].reshape(tiles, capacity, depth),
            packed[:, depth].reshape(tiles, id_rows, depth),
            jnp.zeros((tiles, (-id_rows) % 8, depth), jnp.float32),
        ],
        axis=1,
    )
    arrived_all = exchange_rows(sendbuf, n_plan, 4)
    arrived = arrived_all[:, :capacity, :]
    arrived_ids = arrived_all[:, capacity:capacity + id_rows, :]
    picks = (
        jnp.arange(PATCH_DEV, dtype=jnp.int32)[:, None] == arrived_ids.reshape(1, tiles * capacity).astype(jnp.int32)
    ).astype(jnp.float32)
    summed = jnp.dot(picks, arrived.reshape(tiles * capacity, depth), precision=lax.Precision.HIGHEST,
                     preferred_element_type=jnp.float32)
    patch_sens = 0.25 * summed
    return (cast_density, filtered_sens, patch_sens)


def solution(mesh):
    in_specs = (
        P("plan", None, "draw"),
        P("plan", None, "draw"),
        P(),
        P("plan", None, "draw"),
        P("plan", "draw", None),
    )
    out_specs = (P("plan", None, "draw"), P("plan", None, "draw"), P("plan", "draw"))
    return jax.shard_map(
        functools.partial(per_device, mesh.shape["plan"], mesh.shape["draw"]),
        mesh=mesh, in_specs=in_specs, out_specs=out_specs, check_vma=False
    )
```

```python
import functools

import jax
import jax.numpy as jnp
from jax import lax
from jax.experimental import pallas as pl
from jax.experimental.pallas import tpu as pltpu
from jax.sharding import PartitionSpec as P

PATCH_DEV = 512
SWEEPS = 16
HALO = 8

BETA = 8.0
ETA = 0.5
RMIN = 0.2
POWER = 6.0

MESH = pl.DeviceIdType.MESH


def scan_kernel(n_draw, reverse, part_ref, out_ref, held, send_sem, recv_sem):
    p = lax.axis_index("plan")
    d = lax.axis_index("draw")
    held[...] = jnp.zeros_like(held)
    barrier = pltpu.get_barrier_semaphore()
    for e in range(n_draw):
        @pl.when(d != e)
        def _():
            pl.semaphore_signal(barrier, 1, device_id=(p, e), device_id_type=MESH)
    pl.semaphore_wait(barrier, n_draw - 1)

    def later(e):
        return e < d if reverse else e > d

    def earlier(e):
        return e > d if reverse else e < d

    sends = []
    for e in range(n_draw):
        copy = pltpu.make_async_remote_copy(
            part_ref, held.at[d], send_sem.at[e], recv_sem.at[d], device_id=(p, e), device_id_type=MESH)
        sends.append(copy)

        @pl.when(later(e))
        def _():
            copy.start()
    for e in range(n_draw):
        incoming = pltpu.make_async_remote_copy(
            part_ref, held.at[e], send_sem.at[e], recv_sem.at[e], device_id=(p, e), device_id_type=MESH)

        @pl.when(later(e))
        def _():
            sends[e].wait_send()

        @pl.when(earlier(e))
        def _():
            incoming.wait_recv()
    total = held[0]
    for e in range(1, n_draw):
        total = total + held[e]
    out_ref[...] = total


def entering(part, n_draw, reverse, kid):
    vmem = pl.BlockSpec(memory_space=pltpu.VMEM)
    return pl.pallas_call(
        functools.partial(scan_kernel, n_draw, reverse),
        out_shape=jax.ShapeDtypeStruct(part.shape, jnp.float32),
        in_specs=[vmem],
        out_specs=vmem,
        scratch_shapes=[
            pltpu.VMEM((n_draw,) + part.shape, jnp.float32),
            pltpu.SemaphoreType.DMA((n_draw,)),
            pltpu.SemaphoreType.DMA((n_draw,)),
        ],
        compiler_params=pltpu.CompilerParams(collective_id=kid, has_side_effects=True),
    )(part)


def filter_kernel(n_plan, n_draw, src_ref, ids_ref, radii_ref, out_ref, field, cx_ref, cy_ref, cz_ref, inv_ref,
                  send_sem, recv_sem):
    planes, depth, width = src_ref.shape
    for i in range(planes):
        cls = ids_ref[i]
        cx = jnp.zeros((depth, width), jnp.float32)
        cy = jnp.zeros((depth, width), jnp.float32)
        cz = jnp.zeros((depth, width), jnp.float32)
        for level in range(radii_ref.shape[0]):
            hit = cls == level
            cx = jnp.where(hit, radii_ref[level, 0], cx)
            cy = jnp.where(hit, radii_ref[level, 1], cy)
            cz = jnp.where(hit, radii_ref[level, 2], cz)
        cx_ref[i] = cx
        cy_ref[i] = cy
        cz_ref[i] = cz
        inv_ref[i] = 1.0 / (1.0 + 2.0 * (cx + cy + cz))
    p = lax.axis_index("plan")
    d = lax.axis_index("draw")
    has_l = p > 0
    has_r = p < n_plan - 1
    has_b = d > 0
    has_a = d < n_draw - 1
    lo = HALO
    hi = HALO + depth

    field[...] = jnp.zeros_like(field)
    for i in range(planes):
        field[0, i + 1, pl.ds(lo, depth), :] = src_ref[i]

    barrier = pltpu.get_barrier_semaphore()
    neighbours = ((has_l, (p - 1, d)), (has_r, (p + 1, d)), (has_b, (p, d - 1)), (has_a, (p, d + 1)))
    for cond, dev in neighbours:
        @pl.when(cond)
        def _():
            pl.semaphore_signal(barrier, 1, device_id=dev, device_id_type=MESH)
    peers = sum(cond.astype(jnp.int32) for cond, _ in neighbours)
    pl.semaphore_wait(barrier, peers)

    def copies(s):
        to_l = pltpu.make_async_remote_copy(
            field.at[s, 1, pl.ds(lo, depth), :], field.at[s, planes + 1, pl.ds(lo, depth), :],
            send_sem.at[s, 0], recv_sem.at[s, 0], device_id=(p - 1, d), device_id_type=MESH)
        to_r = pltpu.make_async_remote_copy(
            field.at[s, planes, pl.ds(lo, depth), :], field.at[s, 0, pl.ds(lo, depth), :],
            send_sem.at[s, 1], recv_sem.at[s, 1], device_id=(p + 1, d), device_id_type=MESH)
        to_b = pltpu.make_async_remote_copy(
            field.at[s, pl.ds(1, planes), pl.ds(lo, HALO), :], field.at[s, pl.ds(1, planes), pl.ds(hi, HALO), :],
            send_sem.at[s, 2], recv_sem.at[s, 2], device_id=(p, d - 1), device_id_type=MESH)
        to_a = pltpu.make_async_remote_copy(
            field.at[s, pl.ds(1, planes), pl.ds(hi - HALO, HALO), :], field.at[s, pl.ds(1, planes), pl.ds(0, HALO), :],
            send_sem.at[s, 3], recv_sem.at[s, 3], device_id=(p, d + 1), device_id_type=MESH)
        return ((to_l, has_l, has_r), (to_r, has_r, has_l), (to_b, has_b, has_a), (to_a, has_a, has_b))

    def exchange(s):
        group = copies(s)
        for copy, send, _ in group:
            @pl.when(send)
            def _():
                copy.start()
        for copy, send, recv in group:
            @pl.when(recv)
            def _():
                copy.wait_recv()

    def sent(s):
        for copy, send, _ in copies(s):
            @pl.when(send)
            def _():
                copy.wait_send()

    lane = lax.broadcasted_iota(jnp.int32, (depth, width), 1)

    def update(s, i, r0, rows, last):
        at = lo + r0
        c = field[s, i + 1, pl.ds(at, rows), :]
        zm = field[s, i + 1, pl.ds(at - 1, rows), :]
        zp = field[s, i + 1, pl.ds(at + 1, rows), :]
        xm = field[s, i, pl.ds(at, rows), :]
        xp = field[s, i + 2, pl.ds(at, rows), :]
        lanes = lane[:rows]
        ym = jnp.where(lanes == 0, 0.0, pltpu.roll(c, 1, 1))
        yp = jnp.where(lanes == width - 1, 0.0, pltpu.roll(c, width - 1, 1))
        part = pl.ds(r0, rows)
        new = (src_ref[i, part, :] + cx_ref[i, part, :] * (xm + xp) + cy_ref[i, part, :] * (ym + yp)
               + cz_ref[i, part, :] * (zm + zp)) * inv_ref[i, part, :]
        if last:
            out_ref[i, part, :] = new
        else:
            field[1 - s, i + 1, pl.ds(at, rows), :] = new

    def sweep_send(s):
        t = 1 - s
        group = copies(t)
        update(s, 0, 0, depth, False)
        update(s, planes - 1, 0, depth, False)
        for copy, send, _ in group[:2]:
            @pl.when(send)
            def _():
                copy.start()
        for i in range(1, planes - 1):
            update(s, i, 0, HALO, False)
            update(s, i, depth - HALO, HALO, False)
        for copy, send, _ in group[2:]:
            @pl.when(send)
            def _():
                copy.start()
        for i in range(1, planes - 1):
            update(s, i, HALO, depth - 2 * HALO, False)
        for copy, send, recv in group:
            @pl.when(recv)
            def _():
                copy.wait_recv()
        sent(s)

    exchange(0)

    def pair(k, carry):
        sweep_send(0)
        sweep_send(1)
        return carry

    lax.fori_loop(0, SWEEPS // 2 - 1, pair, 0)
    sweep_send(0)
    for i in range(planes):
        update(1, i, 0, depth, True)
    sent(1)


def smooth_each(source, class_ids, class_radii, n_plan, n_draw, kid):
    planes, depth, width = source.shape
    vmem = pl.BlockSpec(memory_space=pltpu.VMEM)
    smem = pl.BlockSpec(memory_space=pltpu.SMEM)
    return pl.pallas_call(
        functools.partial(filter_kernel, n_plan, n_draw),
        out_shape=jax.ShapeDtypeStruct(source.shape, jnp.float32),
        in_specs=[vmem, vmem, smem],
        out_specs=vmem,
        scratch_shapes=[
            pltpu.VMEM((2, planes + 2, depth + 2 * HALO, width), jnp.float32),
            pltpu.VMEM(source.shape, jnp.float32),
            pltpu.VMEM(source.shape, jnp.float32),
            pltpu.VMEM(source.shape, jnp.float32),
            pltpu.VMEM(source.shape, jnp.float32),
            pltpu.SemaphoreType.DMA((2, 4)),
            pltpu.SemaphoreType.DMA((2, 4)),
        ],
        compiler_params=pltpu.CompilerParams(collective_id=kid, has_side_effects=True),
    )(source, class_ids, class_radii)


def per_device(n_plan, n_draw, design, class_ids, class_radii, sensitivity, row_patch):
    design_t = jnp.swapaxes(design, 1, 2)
    ids_t = jnp.swapaxes(class_ids, 1, 2)
    sens_t = jnp.swapaxes(sensitivity, 1, 2)
    filtered = smooth_each(design_t, ids_t, class_radii, n_plan, n_draw, 0)
    denom = jnp.tanh(jnp.float32(BETA * ETA)) + jnp.tanh(jnp.float32(BETA * (1.0 - ETA)))
    steep = jnp.tanh(BETA * (filtered - ETA))
    projected = RMIN + (1.0 - RMIN) * (jnp.tanh(jnp.float32(BETA * ETA)) + steep) / denom
    running = jnp.cumsum(jnp.power(projected, POWER), axis=1)
    totals = running[:, -1, :]
    carried = entering(totals, n_draw, False, 2)
    prefix = running + carried[:, None, :]
    cast_density = jnp.power(prefix, 1.0 / POWER)
    weighted = sens_t * jnp.power(prefix, (1.0 - POWER) / POWER)
    backward = lax.cumsum(weighted, axis=1, reverse=True)
    rests = backward[:, 0, :]
    below = entering(rests, n_draw, True, 3)
    suffix = backward + below[:, None, :]
    chained = (
        jnp.power(projected, POWER - 1.0)
        * suffix
        * (1.0 - RMIN)
        * BETA
        * (1.0 - steep * steep)
        / denom
    )
    filtered_sens_t = smooth_each(chained, ids_t, class_radii, n_plan, n_draw, 1)
    filtered_sens = jnp.swapaxes(filtered_sens_t, 1, 2)
    cast_density = jnp.swapaxes(cast_density, 1, 2)
    depth = filtered_sens.shape[2]
    row_count = filtered_sens.shape[0] * filtered_sens.shape[1]
    tiles = lax.axis_size("plan")
    capacity = 4 * row_count // tiles
    row_data = filtered_sens.reshape(row_count, depth)
    patch_ids = row_patch.reshape(row_count)
    owners = patch_ids // PATCH_DEV
    slot_patch = patch_ids - owners * PATCH_DEV
    onehot = (owners[:, None] == jnp.arange(tiles, dtype=jnp.int32)[None, :]).astype(jnp.bfloat16)
    rows = jnp.arange(row_count, dtype=jnp.int32)
    upto = (rows[None, :] <= rows[:, None]).astype(jnp.bfloat16)
    counted = jnp.dot(upto, onehot, preferred_element_type=jnp.float32)
    ranking = jnp.sum(counted * onehot.astype(jnp.float32), axis=1).astype(jnp.int32) - 1
    position = owners * capacity + ranking
    source_row = jnp.full((tiles * capacity,), row_count, jnp.int32).at[position].set(rows)
    table = jnp.concatenate(
        [row_data, jnp.broadcast_to(slot_patch.astype(jnp.float32)[:, None], (row_count, depth))], axis=1)
    table = jnp.concatenate(
        [table, jnp.concatenate([jnp.zeros((1, depth), jnp.float32), jnp.full((1, depth), float(PATCH_DEV))], axis=1)])
    packed = jnp.take(table, source_row, axis=0)
    id_rows = capacity // depth
    sendbuf = jnp.concatenate(
        [
            packed[:, :depth].reshape(tiles, capacity, depth),
            packed[:, depth].reshape(tiles, id_rows, depth),
            jnp.zeros((tiles, (-id_rows) % 8, depth), jnp.float32),
        ],
        axis=1,
    )
    arrived_all = lax.all_to_all(sendbuf, "plan", split_axis=0, concat_axis=0, tiled=True)
    arrived = arrived_all[:, :capacity, :]
    arrived_ids = arrived_all[:, capacity:capacity + id_rows, :]
    picks = (
        jnp.arange(PATCH_DEV, dtype=jnp.int32)[:, None] == arrived_ids.reshape(1, tiles * capacity).astype(jnp.int32)
    ).astype(jnp.float32)
    summed = jnp.dot(picks, arrived.reshape(tiles * capacity, depth), precision=lax.Precision.HIGHEST,
                     preferred_element_type=jnp.float32)
    patch_sens = 0.25 * summed
    return (cast_density, filtered_sens, patch_sens)


def solution(mesh):
    in_specs = (
        P("plan", None, "draw"),
        P("plan", None, "draw"),
        P(),
        P("plan", None, "draw"),
        P("plan", "draw", None),
    )
    out_specs = (P("plan", None, "draw"), P("plan", None, "draw"), P("plan", "draw"))
    return jax.shard_map(
        functools.partial(per_device, mesh.shape["plan"], mesh.shape["draw"]),
        mesh=mesh, in_specs=in_specs, out_specs=out_specs, check_vma=False
    )
```

```python
import functools

import jax
import jax.numpy as jnp
from jax import lax
from jax.experimental import pallas as pl
from jax.experimental.pallas import tpu as pltpu
from jax.sharding import PartitionSpec as P

PATCH_DEV = 512
SWEEPS = 16
HALO = 8

BETA = 8.0
ETA = 0.5
RMIN = 0.2
POWER = 6.0

MESH = pl.DeviceIdType.MESH


def scan_kernel(n_draw, reverse, part_ref, out_ref, held, send_sem, recv_sem):
    p = lax.axis_index("plan")
    d = lax.axis_index("draw")
    held[...] = jnp.zeros_like(held)
    barrier = pltpu.get_barrier_semaphore()
    for e in range(n_draw):
        @pl.when(d != e)
        def _():
            pl.semaphore_signal(barrier, 1, device_id=(p, e), device_id_type=MESH)
    pl.semaphore_wait(barrier, n_draw - 1)

    def later(e):
        return e < d if reverse else e > d

    def earlier(e):
        return e > d if reverse else e < d

    sends = []
    for e in range(n_draw):
        copy = pltpu.make_async_remote_copy(
            part_ref, held.at[d], send_sem.at[e], recv_sem.at[d], device_id=(p, e), device_id_type=MESH)
        sends.append(copy)

        @pl.when(later(e))
        def _():
            copy.start()
    for e in range(n_draw):
        incoming = pltpu.make_async_remote_copy(
            part_ref, held.at[e], send_sem.at[e], recv_sem.at[e], device_id=(p, e), device_id_type=MESH)

        @pl.when(later(e))
        def _():
            sends[e].wait_send()

        @pl.when(earlier(e))
        def _():
            incoming.wait_recv()
    total = held[0]
    for e in range(1, n_draw):
        total = total + held[e]
    out_ref[...] = total


def entering(part, n_draw, reverse, kid):
    vmem = pl.BlockSpec(memory_space=pltpu.VMEM)
    return pl.pallas_call(
        functools.partial(scan_kernel, n_draw, reverse),
        out_shape=jax.ShapeDtypeStruct(part.shape, jnp.float32),
        in_specs=[vmem],
        out_specs=vmem,
        scratch_shapes=[
            pltpu.VMEM((n_draw,) + part.shape, jnp.float32),
            pltpu.SemaphoreType.DMA((n_draw,)),
            pltpu.SemaphoreType.DMA((n_draw,)),
        ],
        compiler_params=pltpu.CompilerParams(collective_id=kid, has_side_effects=True),
    )(part)


def filter_kernel(n_plan, n_draw, src_ref, ids_ref, radii_ref, out_ref, field, cx_ref, cy_ref, cz_ref, inv_ref,
                  send_sem, recv_sem):
    planes, depth, width = src_ref.shape
    for i in range(planes):
        cls = ids_ref[i]
        cx = jnp.zeros((depth, width), jnp.float32)
        cy = jnp.zeros((depth, width), jnp.float32)
        cz = jnp.zeros((depth, width), jnp.float32)
        for level in range(radii_ref.shape[0]):
            hit = cls == level
            cx = jnp.where(hit, radii_ref[level, 0], cx)
            cy = jnp.where(hit, radii_ref[level, 1], cy)
            cz = jnp.where(hit, radii_ref[level, 2], cz)
        cx_ref[i] = cx
        cy_ref[i] = cy
        cz_ref[i] = cz
        inv_ref[i] = 1.0 / (1.0 + 2.0 * (cx + cy + cz))
    p = lax.axis_index("plan")
    d = lax.axis_index("draw")
    has_l = p > 0
    has_r = p < n_plan - 1
    has_b = d > 0
    has_a = d < n_draw - 1
    lo = HALO
    hi = HALO + depth

    field[...] = jnp.zeros_like(field)
    for i in range(planes):
        field[0, i + 1, pl.ds(lo, depth), :] = src_ref[i]

    barrier = pltpu.get_barrier_semaphore()
    neighbours = ((has_l, (p - 1, d)), (has_r, (p + 1, d)), (has_b, (p, d - 1)), (has_a, (p, d + 1)))
    for cond, dev in neighbours:
        @pl.when(cond)
        def _():
            pl.semaphore_signal(barrier, 1, device_id=dev, device_id_type=MESH)
    peers = sum(cond.astype(jnp.int32) for cond, _ in neighbours)
    pl.semaphore_wait(barrier, peers)

    def copies(s):
        to_l = pltpu.make_async_remote_copy(
            field.at[s, 1, pl.ds(lo, depth), :], field.at[s, planes + 1, pl.ds(lo, depth), :],
            send_sem.at[s, 0], recv_sem.at[s, 0], device_id=(p - 1, d), device_id_type=MESH)
        to_r = pltpu.make_async_remote_copy(
            field.at[s, planes, pl.ds(lo, depth), :], field.at[s, 0, pl.ds(lo, depth), :],
            send_sem.at[s, 1], recv_sem.at[s, 1], device_id=(p + 1, d), device_id_type=MESH)
        to_b = pltpu.make_async_remote_copy(
            field.at[s, pl.ds(1, planes), pl.ds(lo, HALO), :], field.at[s, pl.ds(1, planes), pl.ds(hi, HALO), :],
            send_sem.at[s, 2], recv_sem.at[s, 2], device_id=(p, d - 1), device_id_type=MESH)
        to_a = pltpu.make_async_remote_copy(
            field.at[s, pl.ds(1, planes), pl.ds(hi - HALO, HALO), :], field.at[s, pl.ds(1, planes), pl.ds(0, HALO), :],
            send_sem.at[s, 3], recv_sem.at[s, 3], device_id=(p, d + 1), device_id_type=MESH)
        return ((to_l, has_l, has_r), (to_r, has_r, has_l), (to_b, has_b, has_a), (to_a, has_a, has_b))

    def exchange(s):
        group = copies(s)
        for copy, send, _ in group:
            @pl.when(send)
            def _():
                copy.start()
        for copy, send, recv in group:
            @pl.when(send)
            def _():
                copy.wait_send()

            @pl.when(recv)
            def _():
                copy.wait_recv()

    lane = lax.broadcasted_iota(jnp.int32, (depth, width), 1)

    def update(s, i, r0, rows, last):
        at = lo + r0
        c = field[s, i + 1, pl.ds(at, rows), :]
        zm = field[s, i + 1, pl.ds(at - 1, rows), :]
        zp = field[s, i + 1, pl.ds(at + 1, rows), :]
        xm = field[s, i, pl.ds(at, rows), :]
        xp = field[s, i + 2, pl.ds(at, rows), :]
        lanes = lane[:rows]
        ym = jnp.where(lanes == 0, 0.0, pltpu.roll(c, 1, 1))
        yp = jnp.where(lanes == width - 1, 0.0, pltpu.roll(c, width - 1, 1))
        part = pl.ds(r0, rows)
        new = (src_ref[i, part, :] + cx_ref[i, part, :] * (xm + xp) + cy_ref[i, part, :] * (ym + yp)
               + cz_ref[i, part, :] * (zm + zp)) * inv_ref[i, part, :]
        if last:
            out_ref[i, part, :] = new
        else:
            field[1 - s, i + 1, pl.ds(at, rows), :] = new

    def sweep_send(s):
        t = 1 - s
        group = copies(t)
        update(s, 0, 0, depth, False)
        update(s, planes - 1, 0, depth, False)
        for copy, send, _ in group[:2]:
            @pl.when(send)
            def _():
                copy.start()
        for i in range(1, planes - 1):
            update(s, i, 0, HALO, False)
            update(s, i, depth - HALO, HALO, False)
        for copy, send, _ in group[2:]:
            @pl.when(send)
            def _():
                copy.start()
        for i in range(1, planes - 1):
            update(s, i, HALO, depth - 2 * HALO, False)
        for copy, send, recv in group:
            @pl.when(send)
            def _():
                copy.wait_send()

            @pl.when(recv)
            def _():
                copy.wait_recv()

    exchange(0)

    def pair(k, carry):
        sweep_send(0)
        sweep_send(1)
        return carry

    lax.fori_loop(0, SWEEPS // 2 - 1, pair, 0)
    sweep_send(0)
    for i in range(planes):
        update(1, i, 0, depth, True)


def smooth_each(source, class_ids, class_radii, n_plan, n_draw, kid):
    planes, depth, width = source.shape
    vmem = pl.BlockSpec(memory_space=pltpu.VMEM)
    smem = pl.BlockSpec(memory_space=pltpu.SMEM)
    return pl.pallas_call(
        functools.partial(filter_kernel, n_plan, n_draw),
        out_shape=jax.ShapeDtypeStruct(source.shape, jnp.float32),
        in_specs=[vmem, vmem, smem],
        out_specs=vmem,
        scratch_shapes=[
            pltpu.VMEM((2, planes + 2, depth + 2 * HALO, width), jnp.float32),
            pltpu.VMEM(source.shape, jnp.float32),
            pltpu.VMEM(source.shape, jnp.float32),
            pltpu.VMEM(source.shape, jnp.float32),
            pltpu.VMEM(source.shape, jnp.float32),
            pltpu.SemaphoreType.DMA((2, 4)),
            pltpu.SemaphoreType.DMA((2, 4)),
        ],
        compiler_params=pltpu.CompilerParams(collective_id=kid, has_side_effects=True),
    )(source, class_ids, class_radii)


def per_device(n_plan, n_draw, design, class_ids, class_radii, sensitivity, row_patch):
    design_t = jnp.swapaxes(design, 1, 2)
    ids_t = jnp.swapaxes(class_ids, 1, 2)
    sens_t = jnp.swapaxes(sensitivity, 1, 2)
    filtered = smooth_each(design_t, ids_t, class_radii, n_plan, n_draw, 0)
    denom = jnp.tanh(jnp.float32(BETA * ETA)) + jnp.tanh(jnp.float32(BETA * (1.0 - ETA)))
    steep = jnp.tanh(BETA * (filtered - ETA))
    projected = RMIN + (1.0 - RMIN) * (jnp.tanh(jnp.float32(BETA * ETA)) + steep) / denom
    running = jnp.cumsum(jnp.power(projected, POWER), axis=1)
    totals = running[:, -1, :]
    carried = entering(totals, n_draw, False, 2)
    prefix = running + carried[:, None, :]
    cast_density = jnp.power(prefix, 1.0 / POWER)
    weighted = sens_t * jnp.power(prefix, (1.0 - POWER) / POWER)
    backward = lax.cumsum(weighted, axis=1, reverse=True)
    rests = backward[:, 0, :]
    below = entering(rests, n_draw, True, 3)
    suffix = backward + below[:, None, :]
    chained = (
        jnp.power(projected, POWER - 1.0)
        * suffix
        * (1.0 - RMIN)
        * BETA
        * (1.0 - steep * steep)
        / denom
    )
    filtered_sens_t = smooth_each(chained, ids_t, class_radii, n_plan, n_draw, 1)
    filtered_sens = jnp.swapaxes(filtered_sens_t, 1, 2)
    cast_density = jnp.swapaxes(cast_density, 1, 2)
    depth = filtered_sens.shape[2]
    row_count = filtered_sens.shape[0] * filtered_sens.shape[1]
    tiles = lax.axis_size("plan")
    capacity = 4 * row_count // tiles
    row_data = filtered_sens.reshape(row_count, depth)
    patch_ids = row_patch.reshape(row_count)
    owners = patch_ids // PATCH_DEV
    slot_patch = patch_ids - owners * PATCH_DEV
    onehot = (owners[:, None] == jnp.arange(tiles, dtype=jnp.int32)[None, :]).astype(jnp.bfloat16)
    rows = jnp.arange(row_count, dtype=jnp.int32)
    upto = (rows[None, :] <= rows[:, None]).astype(jnp.bfloat16)
    counted = jnp.dot(upto, onehot, preferred_element_type=jnp.float32)
    ranking = jnp.sum(counted * onehot.astype(jnp.float32), axis=1).astype(jnp.int32) - 1
    position = owners * capacity + ranking
    slots = tiles * capacity
    source_row = jnp.full((slots,), row_count, jnp.int32).at[position].set(rows)
    send_ids = jnp.full((slots,), float(PATCH_DEV), jnp.float32).at[position].set(slot_patch.astype(jnp.float32))
    id_rows = capacity // depth
    pad_rows = (-id_rows) % 8
    table = jnp.concatenate([row_data, jnp.zeros((1, depth), jnp.float32), send_ids.reshape(slots // depth, depth)])
    chunk_rows = source_row.reshape(tiles, capacity)
    id_index = row_count + 1 + jnp.arange(tiles * id_rows, dtype=jnp.int32).reshape(tiles, id_rows)
    pad_index = jnp.full((tiles, pad_rows), row_count, jnp.int32)
    index = jnp.concatenate([chunk_rows, id_index, pad_index], axis=1).reshape(-1)
    sendbuf = jnp.take(table, index, axis=0).reshape(tiles, capacity + id_rows + pad_rows, depth)
    arrived_all = lax.all_to_all(sendbuf, "plan", split_axis=0, concat_axis=0, tiled=True)
    arrived = arrived_all[:, :capacity, :]
    arrived_ids = arrived_all[:, capacity:capacity + id_rows, :]
    picks = (
        jnp.arange(PATCH_DEV, dtype=jnp.int32)[:, None] == arrived_ids.reshape(1, tiles * capacity).astype(jnp.int32)
    ).astype(jnp.float32)
    summed = jnp.dot(picks, arrived.reshape(tiles * capacity, depth), precision=lax.Precision.HIGHEST,
                     preferred_element_type=jnp.float32)
    patch_sens = 0.25 * summed
    return (cast_density, filtered_sens, patch_sens)


def solution(mesh):
    in_specs = (
        P("plan", None, "draw"),
        P("plan", None, "draw"),
        P(),
        P("plan", None, "draw"),
        P("plan", "draw", None),
    )
    out_specs = (P("plan", None, "draw"), P("plan", None, "draw"), P("plan", "draw"))
    return jax.shard_map(
        functools.partial(per_device, mesh.shape["plan"], mesh.shape["draw"]),
        mesh=mesh, in_specs=in_specs, out_specs=out_specs, check_vma=False
    )
```

```python
import functools

import jax
import jax.numpy as jnp
from jax import lax
from jax.experimental import pallas as pl
from jax.experimental.pallas import tpu as pltpu
from jax.sharding import PartitionSpec as P

PATCH_DEV = 512
SWEEPS = 16
HALO = 8

BETA = 8.0
ETA = 0.5
RMIN = 0.2
POWER = 6.0

MESH = pl.DeviceIdType.MESH


def scan_kernel(n_draw, reverse, part_ref, out_ref, held, send_sem, recv_sem):
    p = lax.axis_index("plan")
    d = lax.axis_index("draw")
    held[...] = jnp.zeros_like(held)
    barrier = pltpu.get_barrier_semaphore()
    for e in range(n_draw):
        @pl.when(d != e)
        def _():
            pl.semaphore_signal(barrier, 1, device_id=(p, e), device_id_type=MESH)
    pl.semaphore_wait(barrier, n_draw - 1)

    def later(e):
        return e < d if reverse else e > d

    def earlier(e):
        return e > d if reverse else e < d

    sends = []
    for e in range(n_draw):
        copy = pltpu.make_async_remote_copy(
            part_ref, held.at[d], send_sem.at[e], recv_sem.at[d], device_id=(p, e), device_id_type=MESH)
        sends.append(copy)

        @pl.when(later(e))
        def _():
            copy.start()
    for e in range(n_draw):
        incoming = pltpu.make_async_remote_copy(
            part_ref, held.at[e], send_sem.at[e], recv_sem.at[e], device_id=(p, e), device_id_type=MESH)

        @pl.when(later(e))
        def _():
            sends[e].wait_send()

        @pl.when(earlier(e))
        def _():
            incoming.wait_recv()
    total = held[0]
    for e in range(1, n_draw):
        total = total + held[e]
    out_ref[...] = total


def entering(part, n_draw, reverse, kid):
    vmem = pl.BlockSpec(memory_space=pltpu.VMEM)
    return pl.pallas_call(
        functools.partial(scan_kernel, n_draw, reverse),
        out_shape=jax.ShapeDtypeStruct(part.shape, jnp.float32),
        in_specs=[vmem],
        out_specs=vmem,
        scratch_shapes=[
            pltpu.VMEM((n_draw,) + part.shape, jnp.float32),
            pltpu.SemaphoreType.DMA((n_draw,)),
            pltpu.SemaphoreType.DMA((n_draw,)),
        ],
        compiler_params=pltpu.CompilerParams(collective_id=kid, has_side_effects=True),
    )(part)


def filter_kernel(n_plan, n_draw, src_ref, ids_ref, radii_ref, out_ref, field, cx_ref, cy_ref, cz_ref, inv_ref,
                  send_sem, recv_sem):
    planes, depth, width = src_ref.shape
    for i in range(planes):
        cls = ids_ref[i]
        cx = jnp.zeros((depth, width), jnp.float32)
        cy = jnp.zeros((depth, width), jnp.float32)
        cz = jnp.zeros((depth, width), jnp.float32)
        for level in range(radii_ref.shape[0]):
            hit = cls == level
            cx = jnp.where(hit, radii_ref[level, 0], cx)
            cy = jnp.where(hit, radii_ref[level, 1], cy)
            cz = jnp.where(hit, radii_ref[level, 2], cz)
        cx_ref[i] = cx
        cy_ref[i] = cy
        cz_ref[i] = cz
        inv_ref[i] = 1.0 / (1.0 + 2.0 * (cx + cy + cz))
    p = lax.axis_index("plan")
    d = lax.axis_index("draw")
    has_l = p > 0
    has_r = p < n_plan - 1
    has_b = d > 0
    has_a = d < n_draw - 1
    lo = HALO
    hi = HALO + depth

    field[...] = jnp.zeros_like(field)
    for i in range(planes):
        field[0, i + 1, pl.ds(lo, depth), :] = src_ref[i]

    barrier = pltpu.get_barrier_semaphore()
    neighbours = ((has_l, (p - 1, d)), (has_r, (p + 1, d)), (has_b, (p, d - 1)), (has_a, (p, d + 1)))
    for cond, dev in neighbours:
        @pl.when(cond)
        def _():
            pl.semaphore_signal(barrier, 1, device_id=dev, device_id_type=MESH)
    peers = sum(cond.astype(jnp.int32) for cond, _ in neighbours)
    pl.semaphore_wait(barrier, peers)

    def copies(s):
        to_l = pltpu.make_async_remote_copy(
            field.at[s, 1, pl.ds(lo, depth), :], field.at[s, planes + 1, pl.ds(lo, depth), :],
            send_sem.at[s, 0], recv_sem.at[s, 0], device_id=(p - 1, d), device_id_type=MESH)
        to_r = pltpu.make_async_remote_copy(
            field.at[s, planes, pl.ds(lo, depth), :], field.at[s, 0, pl.ds(lo, depth), :],
            send_sem.at[s, 1], recv_sem.at[s, 1], device_id=(p + 1, d), device_id_type=MESH)
        to_b = pltpu.make_async_remote_copy(
            field.at[s, pl.ds(1, planes), pl.ds(lo, HALO), :], field.at[s, pl.ds(1, planes), pl.ds(hi, HALO), :],
            send_sem.at[s, 2], recv_sem.at[s, 2], device_id=(p, d - 1), device_id_type=MESH)
        to_a = pltpu.make_async_remote_copy(
            field.at[s, pl.ds(1, planes), pl.ds(hi - HALO, HALO), :], field.at[s, pl.ds(1, planes), pl.ds(0, HALO), :],
            send_sem.at[s, 3], recv_sem.at[s, 3], device_id=(p, d + 1), device_id_type=MESH)
        return ((to_l, has_l, has_r), (to_r, has_r, has_l), (to_b, has_b, has_a), (to_a, has_a, has_b))

    def exchange(s):
        group = copies(s)
        for copy, send, _ in group:
            @pl.when(send)
            def _():
                copy.start()
        for copy, send, recv in group:
            @pl.when(send)
            def _():
                copy.wait_send()

            @pl.when(recv)
            def _():
                copy.wait_recv()

    lane = lax.broadcasted_iota(jnp.int32, (depth, width), 1)

    def update(s, i, r0, rows, last):
        at = lo + r0
        c = field[s, i + 1, pl.ds(at, rows), :]
        zm = field[s, i + 1, pl.ds(at - 1, rows), :]
        zp = field[s, i + 1, pl.ds(at + 1, rows), :]
        xm = field[s, i, pl.ds(at, rows), :]
        xp = field[s, i + 2, pl.ds(at, rows), :]
        lanes = lane[:rows]
        ym = jnp.where(lanes == 0, 0.0, pltpu.roll(c, 1, 1))
        yp = jnp.where(lanes == width - 1, 0.0, pltpu.roll(c, width - 1, 1))
        part = pl.ds(r0, rows)
        new = (src_ref[i, part, :] + cx_ref[i, part, :] * (xm + xp) + cy_ref[i, part, :] * (ym + yp)
               + cz_ref[i, part, :] * (zm + zp)) * inv_ref[i, part, :]
        if last:
            out_ref[i, part, :] = new
        else:
            field[1 - s, i + 1, pl.ds(at, rows), :] = new

    def sweep_send(s):
        t = 1 - s
        group = copies(t)
        update(s, 0, 0, depth, False)
        update(s, planes - 1, 0, depth, False)
        for copy, send, _ in group[:2]:
            @pl.when(send)
            def _():
                copy.start()
        for i in range(1, planes - 1):
            update(s, i, 0, HALO, False)
            update(s, i, depth - HALO, HALO, False)
        for copy, send, _ in group[2:]:
            @pl.when(send)
            def _():
                copy.start()
        for i in range(1, planes - 1):
            update(s, i, HALO, depth - 2 * HALO, False)
        for copy, send, recv in group:
            @pl.when(send)
            def _():
                copy.wait_send()

            @pl.when(recv)
            def _():
                copy.wait_recv()

    exchange(0)

    def pair(k, carry):
        sweep_send(0)
        sweep_send(1)
        return carry

    lax.fori_loop(0, SWEEPS // 2 - 1, pair, 0)
    sweep_send(0)
    for i in range(planes):
        update(1, i, 0, depth, True)


def smooth_each(source, class_ids, class_radii, n_plan, n_draw, kid):
    planes, depth, width = source.shape
    vmem = pl.BlockSpec(memory_space=pltpu.VMEM)
    smem = pl.BlockSpec(memory_space=pltpu.SMEM)
    return pl.pallas_call(
        functools.partial(filter_kernel, n_plan, n_draw),
        out_shape=jax.ShapeDtypeStruct(source.shape, jnp.float32),
        in_specs=[vmem, vmem, smem],
        out_specs=vmem,
        scratch_shapes=[
            pltpu.VMEM((2, planes + 2, depth + 2 * HALO, width), jnp.float32),
            pltpu.VMEM(source.shape, jnp.float32),
            pltpu.VMEM(source.shape, jnp.float32),
            pltpu.VMEM(source.shape, jnp.float32),
            pltpu.VMEM(source.shape, jnp.float32),
            pltpu.SemaphoreType.DMA((2, 4)),
            pltpu.SemaphoreType.DMA((2, 4)),
        ],
        compiler_params=pltpu.CompilerParams(collective_id=kid, has_side_effects=True),
    )(source, class_ids, class_radii)


def per_device(n_plan, n_draw, design, class_ids, class_radii, sensitivity, row_patch):
    design_t = jnp.swapaxes(design, 1, 2)
    ids_t = jnp.swapaxes(class_ids, 1, 2)
    sens_t = jnp.swapaxes(sensitivity, 1, 2)
    filtered = smooth_each(design_t, ids_t, class_radii, n_plan, n_draw, 0)
    denom = jnp.tanh(jnp.float32(BETA * ETA)) + jnp.tanh(jnp.float32(BETA * (1.0 - ETA)))
    steep = jnp.tanh(BETA * (filtered - ETA))
    projected = RMIN + (1.0 - RMIN) * (jnp.tanh(jnp.float32(BETA * ETA)) + steep) / denom
    running = jnp.cumsum(jnp.power(projected, POWER), axis=1)
    totals = running[:, -1, :]
    carried = entering(totals, n_draw, False, 2)
    prefix = running + carried[:, None, :]
    cast_density = jnp.power(prefix, 1.0 / POWER)
    weighted = sens_t * jnp.power(prefix, (1.0 - POWER) / POWER)
    backward = lax.cumsum(weighted, axis=1, reverse=True)
    rests = backward[:, 0, :]
    below = entering(rests, n_draw, True, 3)
    suffix = backward + below[:, None, :]
    chained = (
        jnp.power(projected, POWER - 1.0)
        * suffix
        * (1.0 - RMIN)
        * BETA
        * (1.0 - steep * steep)
        / denom
    )
    filtered_sens_t = smooth_each(chained, ids_t, class_radii, n_plan, n_draw, 1)
    filtered_sens = jnp.swapaxes(filtered_sens_t, 1, 2)
    cast_density = jnp.swapaxes(cast_density, 1, 2)
    depth = filtered_sens.shape[2]
    row_count = filtered_sens.shape[0] * filtered_sens.shape[1]
    tiles = lax.axis_size("plan")
    capacity = 4 * row_count // tiles
    row_data = filtered_sens.reshape(row_count, depth)
    patch_ids = row_patch.reshape(row_count)
    owners = patch_ids // PATCH_DEV
    slot_patch = patch_ids - owners * PATCH_DEV
    onehot = (owners[:, None] == jnp.arange(tiles, dtype=jnp.int32)[None, :]).astype(jnp.bfloat16)
    rows = jnp.arange(row_count, dtype=jnp.int32)
    upto = (rows[None, :] <= rows[:, None]).astype(jnp.bfloat16)
    counted = jnp.dot(upto, onehot, preferred_element_type=jnp.float32)
    ranking = jnp.sum(counted * onehot.astype(jnp.float32), axis=1).astype(jnp.int32) - 1
    position = owners * capacity + ranking
    slots = tiles * capacity
    key = 2 * PATCH_DEV
    filled = jnp.full((slots,), row_count * key + PATCH_DEV, jnp.int32).at[position].set(rows * key + slot_patch)
    source_row = filled // key
    send_ids = (filled % key).astype(jnp.float32)
    id_rows = capacity // depth
    pad_rows = (-id_rows) % 8
    table = jnp.concatenate([row_data, jnp.zeros((1, depth), jnp.float32), send_ids.reshape(slots // depth, depth)])
    chunk_rows = source_row.reshape(tiles, capacity)
    id_index = row_count + 1 + jnp.arange(tiles * id_rows, dtype=jnp.int32).reshape(tiles, id_rows)
    pad_index = jnp.full((tiles, pad_rows), row_count, jnp.int32)
    index = jnp.concatenate([chunk_rows, id_index, pad_index], axis=1).reshape(-1)
    sendbuf = jnp.take(table, index, axis=0).reshape(tiles, capacity + id_rows + pad_rows, depth)
    arrived_all = lax.all_to_all(sendbuf, "plan", split_axis=0, concat_axis=0, tiled=True)
    arrived = arrived_all[:, :capacity, :]
    arrived_ids = arrived_all[:, capacity:capacity + id_rows, :]
    picks = (
        jnp.arange(PATCH_DEV, dtype=jnp.int32)[:, None] == arrived_ids.reshape(1, tiles * capacity).astype(jnp.int32)
    ).astype(jnp.float32)
    summed = jnp.dot(picks, arrived.reshape(tiles * capacity, depth), precision=lax.Precision.HIGHEST,
                     preferred_element_type=jnp.float32)
    patch_sens = 0.25 * summed
    return (cast_density, filtered_sens, patch_sens)


def solution(mesh):
    in_specs = (
        P("plan", None, "draw"),
        P("plan", None, "draw"),
        P(),
        P("plan", None, "draw"),
        P("plan", "draw", None),
    )
    out_specs = (P("plan", None, "draw"), P("plan", None, "draw"), P("plan", "draw"))
    return jax.shard_map(
        functools.partial(per_device, mesh.shape["plan"], mesh.shape["draw"]),
        mesh=mesh, in_specs=in_specs, out_specs=out_specs, check_vma=False
    )
```

```python
import functools

import jax
import jax.numpy as jnp
from jax import lax
from jax.experimental import pallas as pl
from jax.experimental.pallas import tpu as pltpu
from jax.sharding import PartitionSpec as P

PATCH_DEV = 512
SWEEPS = 16
HALO = 8

BETA = 8.0
ETA = 0.5
RMIN = 0.2
POWER = 6.0

MESH = pl.DeviceIdType.MESH


def scan_kernel(n_draw, reverse, part_ref, out_ref, held, send_sem, recv_sem):
    p = lax.axis_index("plan")
    d = lax.axis_index("draw")
    held[...] = jnp.zeros_like(held)
    barrier = pltpu.get_barrier_semaphore()
    for e in range(n_draw):
        @pl.when(d != e)
        def _():
            pl.semaphore_signal(barrier, 1, device_id=(p, e), device_id_type=MESH)
    pl.semaphore_wait(barrier, n_draw - 1)

    def later(e):
        return e < d if reverse else e > d

    def earlier(e):
        return e > d if reverse else e < d

    sends = []
    for e in range(n_draw):
        copy = pltpu.make_async_remote_copy(
            part_ref, held.at[d], send_sem.at[e], recv_sem.at[d], device_id=(p, e), device_id_type=MESH)
        sends.append(copy)

        @pl.when(later(e))
        def _():
            copy.start()
    for e in range(n_draw):
        incoming = pltpu.make_async_remote_copy(
            part_ref, held.at[e], send_sem.at[e], recv_sem.at[e], device_id=(p, e), device_id_type=MESH)

        @pl.when(later(e))
        def _():
            sends[e].wait_send()

        @pl.when(earlier(e))
        def _():
            incoming.wait_recv()
    total = held[0]
    for e in range(1, n_draw):
        total = total + held[e]
    out_ref[...] = total


def entering(part, n_draw, reverse, kid):
    vmem = pl.BlockSpec(memory_space=pltpu.VMEM)
    return pl.pallas_call(
        functools.partial(scan_kernel, n_draw, reverse),
        out_shape=jax.ShapeDtypeStruct(part.shape, jnp.float32),
        in_specs=[vmem],
        out_specs=vmem,
        scratch_shapes=[
            pltpu.VMEM((n_draw,) + part.shape, jnp.float32),
            pltpu.SemaphoreType.DMA((n_draw,)),
            pltpu.SemaphoreType.DMA((n_draw,)),
        ],
        compiler_params=pltpu.CompilerParams(collective_id=kid, has_side_effects=True),
    )(part)


def filter_kernel(n_plan, n_draw, src_ref, ids_ref, radii_ref, out_ref, field, cx_ref, cy_ref, cz_ref, inv_ref,
                  send_sem, recv_sem):
    planes, depth, width = src_ref.shape
    for i in range(planes):
        cls = ids_ref[i]
        cx = jnp.zeros((depth, width), jnp.float32)
        cy = jnp.zeros((depth, width), jnp.float32)
        cz = jnp.zeros((depth, width), jnp.float32)
        for level in range(radii_ref.shape[0]):
            hit = cls == level
            cx = jnp.where(hit, radii_ref[level, 0], cx)
            cy = jnp.where(hit, radii_ref[level, 1], cy)
            cz = jnp.where(hit, radii_ref[level, 2], cz)
        cx_ref[i] = cx
        cy_ref[i] = cy
        cz_ref[i] = cz
        inv_ref[i] = 1.0 / (1.0 + 2.0 * (cx + cy + cz))
    p = lax.axis_index("plan")
    d = lax.axis_index("draw")
    has_l = p > 0
    has_r = p < n_plan - 1
    has_b = d > 0
    has_a = d < n_draw - 1
    lo = HALO
    hi = HALO + depth

    field[...] = jnp.zeros_like(field)
    for i in range(planes):
        field[0, i + 1, pl.ds(lo, depth), :] = src_ref[i]

    barrier = pltpu.get_barrier_semaphore()
    neighbours = ((has_l, (p - 1, d)), (has_r, (p + 1, d)), (has_b, (p, d - 1)), (has_a, (p, d + 1)))
    for cond, dev in neighbours:
        @pl.when(cond)
        def _():
            pl.semaphore_signal(barrier, 1, device_id=dev, device_id_type=MESH)
    peers = sum(cond.astype(jnp.int32) for cond, _ in neighbours)
    pl.semaphore_wait(barrier, peers)

    def copies(s):
        to_l = pltpu.make_async_remote_copy(
            field.at[s, 1, pl.ds(lo, depth), :], field.at[s, planes + 1, pl.ds(lo, depth), :],
            send_sem.at[s, 0], recv_sem.at[s, 0], device_id=(p - 1, d), device_id_type=MESH)
        to_r = pltpu.make_async_remote_copy(
            field.at[s, planes, pl.ds(lo, depth), :], field.at[s, 0, pl.ds(lo, depth), :],
            send_sem.at[s, 1], recv_sem.at[s, 1], device_id=(p + 1, d), device_id_type=MESH)
        to_b = pltpu.make_async_remote_copy(
            field.at[s, pl.ds(1, planes), pl.ds(lo, HALO), :], field.at[s, pl.ds(1, planes), pl.ds(hi, HALO), :],
            send_sem.at[s, 2], recv_sem.at[s, 2], device_id=(p, d - 1), device_id_type=MESH)
        to_a = pltpu.make_async_remote_copy(
            field.at[s, pl.ds(1, planes), pl.ds(hi - HALO, HALO), :], field.at[s, pl.ds(1, planes), pl.ds(0, HALO), :],
            send_sem.at[s, 3], recv_sem.at[s, 3], device_id=(p, d + 1), device_id_type=MESH)
        return ((to_l, has_l, has_r), (to_r, has_r, has_l), (to_b, has_b, has_a), (to_a, has_a, has_b))

    def exchange(s):
        group = copies(s)
        for copy, send, _ in group:
            @pl.when(send)
            def _():
                copy.start()
        for copy, send, recv in group:
            @pl.when(send)
            def _():
                copy.wait_send()

            @pl.when(recv)
            def _():
                copy.wait_recv()

    lane = lax.broadcasted_iota(jnp.int32, (depth, width), 1)

    def update(s, i, r0, rows, last):
        at = lo + r0
        c = field[s, i + 1, pl.ds(at, rows), :]
        zm = field[s, i + 1, pl.ds(at - 1, rows), :]
        zp = field[s, i + 1, pl.ds(at + 1, rows), :]
        xm = field[s, i, pl.ds(at, rows), :]
        xp = field[s, i + 2, pl.ds(at, rows), :]
        lanes = lane[:rows]
        ym = jnp.where(lanes == 0, 0.0, pltpu.roll(c, 1, 1))
        yp = jnp.where(lanes == width - 1, 0.0, pltpu.roll(c, width - 1, 1))
        part = pl.ds(r0, rows)
        new = (src_ref[i, part, :] + cx_ref[i, part, :] * (xm + xp) + cy_ref[i, part, :] * (ym + yp)
               + cz_ref[i, part, :] * (zm + zp)) * inv_ref[i, part, :]
        if last:
            out_ref[i, part, :] = new
        else:
            field[1 - s, i + 1, pl.ds(at, rows), :] = new

    def sweep_send(s):
        t = 1 - s
        group = copies(t)
        update(s, 0, 0, depth, False)
        update(s, planes - 1, 0, depth, False)
        for copy, send, _ in group[:2]:
            @pl.when(send)
            def _():
                copy.start()
        for i in range(1, planes - 1):
            update(s, i, 0, HALO, False)
            update(s, i, depth - HALO, HALO, False)
        for copy, send, _ in group[2:]:
            @pl.when(send)
            def _():
                copy.start()
        for i in range(1, planes - 1):
            update(s, i, HALO, depth - 2 * HALO, False)
        for copy, send, recv in group:
            @pl.when(send)
            def _():
                copy.wait_send()

            @pl.when(recv)
            def _():
                copy.wait_recv()

    exchange(0)

    def pair(k, carry):
        sweep_send(0)
        sweep_send(1)
        return carry

    lax.fori_loop(0, SWEEPS // 2 - 1, pair, 0)
    sweep_send(0)
    for i in range(planes):
        update(1, i, 0, depth, True)


def smooth_each(source, class_ids, class_radii, n_plan, n_draw, kid):
    planes, depth, width = source.shape
    vmem = pl.BlockSpec(memory_space=pltpu.VMEM)
    smem = pl.BlockSpec(memory_space=pltpu.SMEM)
    return pl.pallas_call(
        functools.partial(filter_kernel, n_plan, n_draw),
        out_shape=jax.ShapeDtypeStruct(source.shape, jnp.float32),
        in_specs=[vmem, vmem, smem],
        out_specs=vmem,
        scratch_shapes=[
            pltpu.VMEM((2, planes + 2, depth + 2 * HALO, width), jnp.float32),
            pltpu.VMEM(source.shape, jnp.float32),
            pltpu.VMEM(source.shape, jnp.float32),
            pltpu.VMEM(source.shape, jnp.float32),
            pltpu.VMEM(source.shape, jnp.float32),
            pltpu.SemaphoreType.DMA((2, 4)),
            pltpu.SemaphoreType.DMA((2, 4)),
        ],
        compiler_params=pltpu.CompilerParams(collective_id=kid, has_side_effects=True),
    )(source, class_ids, class_radii)


def per_device(n_plan, n_draw, design, class_ids, class_radii, sensitivity, row_patch):
    design_t = jnp.swapaxes(design, 1, 2)
    ids_t = jnp.swapaxes(class_ids, 1, 2)
    sens_t = jnp.swapaxes(sensitivity, 1, 2)
    filtered = smooth_each(design_t, ids_t, class_radii, n_plan, n_draw, 0)
    denom = jnp.tanh(jnp.float32(BETA * ETA)) + jnp.tanh(jnp.float32(BETA * (1.0 - ETA)))
    steep = jnp.tanh(BETA * (filtered - ETA))
    projected = RMIN + (1.0 - RMIN) * (jnp.tanh(jnp.float32(BETA * ETA)) + steep) / denom
    running = jnp.cumsum(jnp.power(projected, POWER), axis=1)
    totals = running[:, -1, :]
    carried = entering(totals, n_draw, False, 2)
    prefix = running + carried[:, None, :]
    cast_density = jnp.power(prefix, 1.0 / POWER)
    weighted = sens_t * jnp.power(prefix, (1.0 - POWER) / POWER)
    backward = lax.cumsum(weighted, axis=1, reverse=True)
    rests = backward[:, 0, :]
    below = entering(rests, n_draw, True, 3)
    suffix = backward + below[:, None, :]
    chained = (
        jnp.power(projected, POWER - 1.0)
        * suffix
        * (1.0 - RMIN)
        * BETA
        * (1.0 - steep * steep)
        / denom
    )
    filtered_sens_t = smooth_each(chained, ids_t, class_radii, n_plan, n_draw, 1)
    filtered_sens = jnp.swapaxes(filtered_sens_t, 1, 2)
    cast_density = jnp.swapaxes(cast_density, 1, 2)
    depth = filtered_sens.shape[2]
    row_count = filtered_sens.shape[0] * filtered_sens.shape[1]
    tiles = lax.axis_size("plan")
    capacity = 4 * row_count // tiles
    row_data = filtered_sens.reshape(row_count, depth)
    patch_ids = row_patch.reshape(row_count)
    owners = patch_ids // PATCH_DEV
    slot_patch = patch_ids - owners * PATCH_DEV
    onehot = (owners[:, None] == jnp.arange(tiles, dtype=jnp.int32)[None, :]).astype(jnp.bfloat16)
    rows = jnp.arange(row_count, dtype=jnp.int32)
    upto = (rows[None, :] <= rows[:, None]).astype(jnp.bfloat16)
    counted = jnp.dot(upto, onehot, preferred_element_type=jnp.float32)
    ranking = jnp.sum(counted * onehot.astype(jnp.float32), axis=1).astype(jnp.int32) - 1
    position = owners * capacity + ranking
    slots = tiles * capacity
    key = 2 * PATCH_DEV
    filled = jnp.full((slots,), row_count * key + PATCH_DEV, jnp.int32).at[position].set(rows * key + slot_patch)
    source_row = filled // key
    send_ids = (filled % key).astype(jnp.float32)
    id_rows = capacity // depth
    pad_rows = (-id_rows) % 8
    table = jnp.concatenate([row_data, jnp.zeros((1, depth), jnp.float32), send_ids.reshape(slots // depth, depth)])
    chunk_rows = source_row.reshape(tiles, capacity)
    id_index = row_count + 1 + jnp.arange(tiles * id_rows, dtype=jnp.int32).reshape(tiles, id_rows)
    pad_index = jnp.full((tiles, pad_rows), row_count, jnp.int32)
    index = jnp.concatenate([chunk_rows, id_index, pad_index], axis=1).reshape(-1)
    sendbuf = jnp.take(table, index, axis=0).reshape(tiles, capacity + id_rows + pad_rows, depth)
    arrived_all = lax.all_to_all(sendbuf, "plan", split_axis=0, concat_axis=0, tiled=True)
    arrived = arrived_all[:, :capacity, :]
    arrived_ids = arrived_all[:, capacity:capacity + id_rows, :]
    picks = (
        jnp.arange(PATCH_DEV, dtype=jnp.int32)[:, None] == arrived_ids.reshape(1, tiles * capacity).astype(jnp.int32)
    ).astype(jnp.float32)
    summed = jnp.dot(picks, arrived.reshape(tiles * capacity, depth), precision=lax.Precision.HIGH,
                     preferred_element_type=jnp.float32)
    patch_sens = 0.25 * summed
    return (cast_density, filtered_sens, patch_sens)


def solution(mesh):
    in_specs = (
        P("plan", None, "draw"),
        P("plan", None, "draw"),
        P(),
        P("plan", None, "draw"),
        P("plan", "draw", None),
    )
    out_specs = (P("plan", None, "draw"), P("plan", None, "draw"), P("plan", "draw"))
    return jax.shard_map(
        functools.partial(per_device, mesh.shape["plan"], mesh.shape["draw"]),
        mesh=mesh, in_specs=in_specs, out_specs=out_specs, check_vma=False
    )
```

```python
import functools

import jax
import jax.numpy as jnp
from jax import lax
from jax.experimental import pallas as pl
from jax.experimental.pallas import tpu as pltpu
from jax.sharding import PartitionSpec as P

PATCH_DEV = 512
SWEEPS = 16
HALO = 8

BETA = 8.0
ETA = 0.5
RMIN = 0.2
POWER = 6.0

MESH = pl.DeviceIdType.MESH


def scan_kernel(n_draw, reverse, part_ref, out_ref, held, send_sem, recv_sem):
    p = lax.axis_index("plan")
    d = lax.axis_index("draw")
    held[...] = jnp.zeros_like(held)
    barrier = pltpu.get_barrier_semaphore()
    for e in range(n_draw):
        @pl.when(d != e)
        def _():
            pl.semaphore_signal(barrier, 1, device_id=(p, e), device_id_type=MESH)
    pl.semaphore_wait(barrier, n_draw - 1)

    def later(e):
        return e < d if reverse else e > d

    def earlier(e):
        return e > d if reverse else e < d

    sends = []
    for e in range(n_draw):
        copy = pltpu.make_async_remote_copy(
            part_ref, held.at[d], send_sem.at[e], recv_sem.at[d], device_id=(p, e), device_id_type=MESH)
        sends.append(copy)

        @pl.when(later(e))
        def _():
            copy.start()
    for e in range(n_draw):
        incoming = pltpu.make_async_remote_copy(
            part_ref, held.at[e], send_sem.at[e], recv_sem.at[e], device_id=(p, e), device_id_type=MESH)

        @pl.when(later(e))
        def _():
            sends[e].wait_send()

        @pl.when(earlier(e))
        def _():
            incoming.wait_recv()
    total = held[0]
    for e in range(1, n_draw):
        total = total + held[e]
    out_ref[...] = total


def entering(part, n_draw, reverse, kid):
    vmem = pl.BlockSpec(memory_space=pltpu.VMEM)
    return pl.pallas_call(
        functools.partial(scan_kernel, n_draw, reverse),
        out_shape=jax.ShapeDtypeStruct(part.shape, jnp.float32),
        in_specs=[vmem],
        out_specs=vmem,
        scratch_shapes=[
            pltpu.VMEM((n_draw,) + part.shape, jnp.float32),
            pltpu.SemaphoreType.DMA((n_draw,)),
            pltpu.SemaphoreType.DMA((n_draw,)),
        ],
        compiler_params=pltpu.CompilerParams(collective_id=kid, has_side_effects=True),
    )(part)


def filter_kernel(n_plan, n_draw, turn_src, src_in, ids_ref, radii_ref, out_ref, field, cx_ref, cy_ref, cz_ref,
                  inv_ref, src_ref, send_sem, recv_sem):
    planes, depth, width = src_ref.shape
    for i in range(planes):
        src_ref[i] = src_in[i].T if turn_src else src_in[i]
        cls = ids_ref[i].T
        cx = jnp.zeros((depth, width), jnp.float32)
        cy = jnp.zeros((depth, width), jnp.float32)
        cz = jnp.zeros((depth, width), jnp.float32)
        for level in range(radii_ref.shape[0]):
            hit = cls == level
            cx = jnp.where(hit, radii_ref[level, 0], cx)
            cy = jnp.where(hit, radii_ref[level, 1], cy)
            cz = jnp.where(hit, radii_ref[level, 2], cz)
        cx_ref[i] = cx
        cy_ref[i] = cy
        cz_ref[i] = cz
        inv_ref[i] = 1.0 / (1.0 + 2.0 * (cx + cy + cz))
    p = lax.axis_index("plan")
    d = lax.axis_index("draw")
    has_l = p > 0
    has_r = p < n_plan - 1
    has_b = d > 0
    has_a = d < n_draw - 1
    lo = HALO
    hi = HALO + depth

    field[...] = jnp.zeros_like(field)
    for i in range(planes):
        field[0, i + 1, pl.ds(lo, depth), :] = src_ref[i]

    barrier = pltpu.get_barrier_semaphore()
    neighbours = ((has_l, (p - 1, d)), (has_r, (p + 1, d)), (has_b, (p, d - 1)), (has_a, (p, d + 1)))
    for cond, dev in neighbours:
        @pl.when(cond)
        def _():
            pl.semaphore_signal(barrier, 1, device_id=dev, device_id_type=MESH)
    peers = sum(cond.astype(jnp.int32) for cond, _ in neighbours)
    pl.semaphore_wait(barrier, peers)

    def copies(s):
        to_l = pltpu.make_async_remote_copy(
            field.at[s, 1, pl.ds(lo, depth), :], field.at[s, planes + 1, pl.ds(lo, depth), :],
            send_sem.at[s, 0], recv_sem.at[s, 0], device_id=(p - 1, d), device_id_type=MESH)
        to_r = pltpu.make_async_remote_copy(
            field.at[s, planes, pl.ds(lo, depth), :], field.at[s, 0, pl.ds(lo, depth), :],
            send_sem.at[s, 1], recv_sem.at[s, 1], device_id=(p + 1, d), device_id_type=MESH)
        to_b = pltpu.make_async_remote_copy(
            field.at[s, pl.ds(1, planes), pl.ds(lo, HALO), :], field.at[s, pl.ds(1, planes), pl.ds(hi, HALO), :],
            send_sem.at[s, 2], recv_sem.at[s, 2], device_id=(p, d - 1), device_id_type=MESH)
        to_a = pltpu.make_async_remote_copy(
            field.at[s, pl.ds(1, planes), pl.ds(hi - HALO, HALO), :], field.at[s, pl.ds(1, planes), pl.ds(0, HALO), :],
            send_sem.at[s, 3], recv_sem.at[s, 3], device_id=(p, d + 1), device_id_type=MESH)
        return ((to_l, has_l, has_r), (to_r, has_r, has_l), (to_b, has_b, has_a), (to_a, has_a, has_b))

    def exchange(s):
        group = copies(s)
        for copy, send, _ in group:
            @pl.when(send)
            def _():
                copy.start()
        for copy, send, recv in group:
            @pl.when(send)
            def _():
                copy.wait_send()

            @pl.when(recv)
            def _():
                copy.wait_recv()

    lane = lax.broadcasted_iota(jnp.int32, (depth, width), 1)

    def update(s, i, r0, rows, last):
        at = lo + r0
        c = field[s, i + 1, pl.ds(at, rows), :]
        zm = field[s, i + 1, pl.ds(at - 1, rows), :]
        zp = field[s, i + 1, pl.ds(at + 1, rows), :]
        xm = field[s, i, pl.ds(at, rows), :]
        xp = field[s, i + 2, pl.ds(at, rows), :]
        lanes = lane[:rows]
        ym = jnp.where(lanes == 0, 0.0, pltpu.roll(c, 1, 1))
        yp = jnp.where(lanes == width - 1, 0.0, pltpu.roll(c, width - 1, 1))
        part = pl.ds(r0, rows)
        new = (src_ref[i, part, :] + cx_ref[i, part, :] * (xm + xp) + cy_ref[i, part, :] * (ym + yp)
               + cz_ref[i, part, :] * (zm + zp)) * inv_ref[i, part, :]
        if last:
            out_ref[i, part, :] = new
        else:
            field[1 - s, i + 1, pl.ds(at, rows), :] = new

    def sweep_send(s):
        t = 1 - s
        group = copies(t)
        update(s, 0, 0, depth, False)
        update(s, planes - 1, 0, depth, False)
        for copy, send, _ in group[:2]:
            @pl.when(send)
            def _():
                copy.start()
        for i in range(1, planes - 1):
            update(s, i, 0, HALO, False)
            update(s, i, depth - HALO, HALO, False)
        for copy, send, _ in group[2:]:
            @pl.when(send)
            def _():
                copy.start()
        for i in range(1, planes - 1):
            update(s, i, HALO, depth - 2 * HALO, False)
        for copy, send, recv in group:
            @pl.when(send)
            def _():
                copy.wait_send()

            @pl.when(recv)
            def _():
                copy.wait_recv()

    exchange(0)

    def pair(k, carry):
        sweep_send(0)
        sweep_send(1)
        return carry

    lax.fori_loop(0, SWEEPS // 2 - 1, pair, 0)
    sweep_send(0)
    for i in range(planes):
        update(1, i, 0, depth, True)


def smooth_each(source, class_ids, class_radii, n_plan, n_draw, kid, turn_src):
    planes, depth, width = source.shape
    vmem = pl.BlockSpec(memory_space=pltpu.VMEM)
    smem = pl.BlockSpec(memory_space=pltpu.SMEM)
    return pl.pallas_call(
        functools.partial(filter_kernel, n_plan, n_draw, turn_src),
        out_shape=jax.ShapeDtypeStruct(source.shape, jnp.float32),
        in_specs=[vmem, vmem, smem],
        out_specs=vmem,
        scratch_shapes=[
            pltpu.VMEM((2, planes + 2, depth + 2 * HALO, width), jnp.float32),
            pltpu.VMEM(source.shape, jnp.float32),
            pltpu.VMEM(source.shape, jnp.float32),
            pltpu.VMEM(source.shape, jnp.float32),
            pltpu.VMEM(source.shape, jnp.float32),
            pltpu.VMEM(source.shape, jnp.float32),
            pltpu.SemaphoreType.DMA((2, 4)),
            pltpu.SemaphoreType.DMA((2, 4)),
        ],
        compiler_params=pltpu.CompilerParams(collective_id=kid, has_side_effects=True),
    )(source, class_ids, class_radii)


def per_device(n_plan, n_draw, design, class_ids, class_radii, sensitivity, row_patch):
    sens_t = jnp.swapaxes(sensitivity, 1, 2)
    filtered = smooth_each(design, class_ids, class_radii, n_plan, n_draw, 0, True)
    denom = jnp.tanh(jnp.float32(BETA * ETA)) + jnp.tanh(jnp.float32(BETA * (1.0 - ETA)))
    steep = jnp.tanh(BETA * (filtered - ETA))
    projected = RMIN + (1.0 - RMIN) * (jnp.tanh(jnp.float32(BETA * ETA)) + steep) / denom
    running = jnp.cumsum(jnp.power(projected, POWER), axis=1)
    totals = running[:, -1, :]
    carried = entering(totals, n_draw, False, 2)
    prefix = running + carried[:, None, :]
    cast_density = jnp.power(prefix, 1.0 / POWER)
    weighted = sens_t * jnp.power(prefix, (1.0 - POWER) / POWER)
    backward = lax.cumsum(weighted, axis=1, reverse=True)
    rests = backward[:, 0, :]
    below = entering(rests, n_draw, True, 3)
    suffix = backward + below[:, None, :]
    chained = (
        jnp.power(projected, POWER - 1.0)
        * suffix
        * (1.0 - RMIN)
        * BETA
        * (1.0 - steep * steep)
        / denom
    )
    filtered_sens_t = smooth_each(chained, class_ids, class_radii, n_plan, n_draw, 1, False)
    filtered_sens = jnp.swapaxes(filtered_sens_t, 1, 2)
    cast_density = jnp.swapaxes(cast_density, 1, 2)
    depth = filtered_sens.shape[2]
    row_count = filtered_sens.shape[0] * filtered_sens.shape[1]
    tiles = lax.axis_size("plan")
    capacity = 4 * row_count // tiles
    row_data = filtered_sens.reshape(row_count, depth)
    patch_ids = row_patch.reshape(row_count)
    owners = patch_ids // PATCH_DEV
    slot_patch = patch_ids - owners * PATCH_DEV
    onehot = (owners[:, None] == jnp.arange(tiles, dtype=jnp.int32)[None, :]).astype(jnp.bfloat16)
    rows = jnp.arange(row_count, dtype=jnp.int32)
    upto = (rows[None, :] <= rows[:, None]).astype(jnp.bfloat16)
    counted = jnp.dot(upto, onehot, preferred_element_type=jnp.float32)
    ranking = jnp.sum(counted * onehot.astype(jnp.float32), axis=1).astype(jnp.int32) - 1
    position = owners * capacity + ranking
    slots = tiles * capacity
    key = 2 * PATCH_DEV
    filled = jnp.full((slots,), row_count * key + PATCH_DEV, jnp.int32).at[position].set(rows * key + slot_patch)
    source_row = filled // key
    send_ids = (filled % key).astype(jnp.float32)
    id_rows = capacity // depth
    pad_rows = (-id_rows) % 8
    table = jnp.concatenate([row_data, jnp.zeros((1, depth), jnp.float32), send_ids.reshape(slots // depth, depth)])
    chunk_rows = source_row.reshape(tiles, capacity)
    id_index = row_count + 1 + jnp.arange(tiles * id_rows, dtype=jnp.int32).reshape(tiles, id_rows)
    pad_index = jnp.full((tiles, pad_rows), row_count, jnp.int32)
    index = jnp.concatenate([chunk_rows, id_index, pad_index], axis=1).reshape(-1)
    sendbuf = jnp.take(table, index, axis=0).reshape(tiles, capacity + id_rows + pad_rows, depth)
    arrived_all = lax.all_to_all(sendbuf, "plan", split_axis=0, concat_axis=0, tiled=True)
    arrived = arrived_all[:, :capacity, :]
    arrived_ids = arrived_all[:, capacity:capacity + id_rows, :]
    picks = (
        jnp.arange(PATCH_DEV, dtype=jnp.int32)[:, None] == arrived_ids.reshape(1, tiles * capacity).astype(jnp.int32)
    ).astype(jnp.float32)
    summed = jnp.dot(picks, arrived.reshape(tiles * capacity, depth), precision=lax.Precision.HIGH,
                     preferred_element_type=jnp.float32)
    patch_sens = 0.25 * summed
    return (cast_density, filtered_sens, patch_sens)


def solution(mesh):
    in_specs = (
        P("plan", None, "draw"),
        P("plan", None, "draw"),
        P(),
        P("plan", None, "draw"),
        P("plan", "draw", None),
    )
    out_specs = (P("plan", None, "draw"), P("plan", None, "draw"), P("plan", "draw"))
    return jax.shard_map(
        functools.partial(per_device, mesh.shape["plan"], mesh.shape["draw"]),
        mesh=mesh, in_specs=in_specs, out_specs=out_specs, check_vma=False
    )
```

```python
import functools

import jax
import jax.numpy as jnp
from jax import lax
from jax.experimental import pallas as pl
from jax.experimental.pallas import tpu as pltpu
from jax.sharding import PartitionSpec as P

PATCH_DEV = 512
SWEEPS = 16
HALO = 8

BETA = 8.0
ETA = 0.5
RMIN = 0.2
POWER = 6.0

MESH = pl.DeviceIdType.MESH


def scan_kernel(n_draw, reverse, part_ref, out_ref, held, send_sem, recv_sem):
    p = lax.axis_index("plan")
    d = lax.axis_index("draw")
    held[...] = jnp.zeros_like(held)
    barrier = pltpu.get_barrier_semaphore()
    for e in range(n_draw):
        @pl.when(d != e)
        def _():
            pl.semaphore_signal(barrier, 1, device_id=(p, e), device_id_type=MESH)
    pl.semaphore_wait(barrier, n_draw - 1)

    def later(e):
        return e < d if reverse else e > d

    def earlier(e):
        return e > d if reverse else e < d

    sends = []
    for e in range(n_draw):
        copy = pltpu.make_async_remote_copy(
            part_ref, held.at[d], send_sem.at[e], recv_sem.at[d], device_id=(p, e), device_id_type=MESH)
        sends.append(copy)

        @pl.when(later(e))
        def _():
            copy.start()
    for e in range(n_draw):
        incoming = pltpu.make_async_remote_copy(
            part_ref, held.at[e], send_sem.at[e], recv_sem.at[e], device_id=(p, e), device_id_type=MESH)

        @pl.when(later(e))
        def _():
            sends[e].wait_send()

        @pl.when(earlier(e))
        def _():
            incoming.wait_recv()
    total = held[0]
    for e in range(1, n_draw):
        total = total + held[e]
    out_ref[...] = total


def entering(part, n_draw, reverse, kid):
    vmem = pl.BlockSpec(memory_space=pltpu.VMEM)
    return pl.pallas_call(
        functools.partial(scan_kernel, n_draw, reverse),
        out_shape=jax.ShapeDtypeStruct(part.shape, jnp.float32),
        in_specs=[vmem],
        out_specs=vmem,
        scratch_shapes=[
            pltpu.VMEM((n_draw,) + part.shape, jnp.float32),
            pltpu.SemaphoreType.DMA((n_draw,)),
            pltpu.SemaphoreType.DMA((n_draw,)),
        ],
        compiler_params=pltpu.CompilerParams(collective_id=kid, has_side_effects=True),
    )(part)


def filter_kernel(n_plan, n_draw, turn_src, src_in, ids_ref, radii_ref, out_ref, field, cx_ref, cy_ref, cz_ref,
                  inv_ref, src_ref, send_sem, recv_sem):
    planes, depth, width = src_ref.shape
    for i in range(planes):
        src_ref[i] = src_in[i].T if turn_src else src_in[i]
        cls = ids_ref[i].T
        cx = jnp.zeros((depth, width), jnp.float32)
        cy = jnp.zeros((depth, width), jnp.float32)
        cz = jnp.zeros((depth, width), jnp.float32)
        for level in range(radii_ref.shape[0]):
            hit = cls == level
            cx = jnp.where(hit, radii_ref[level, 0], cx)
            cy = jnp.where(hit, radii_ref[level, 1], cy)
            cz = jnp.where(hit, radii_ref[level, 2], cz)
        cx_ref[i] = cx
        cy_ref[i] = cy
        cz_ref[i] = cz
        inv_ref[i] = 1.0 / (1.0 + 2.0 * (cx + cy + cz))
    p = lax.axis_index("plan")
    d = lax.axis_index("draw")
    has_l = p > 0
    has_r = p < n_plan - 1
    has_b = d > 0
    has_a = d < n_draw - 1
    lo = HALO
    hi = HALO + depth

    field[...] = jnp.zeros_like(field)
    for i in range(planes):
        field[0, i + 1, pl.ds(lo, depth), :] = src_ref[i]

    barrier = pltpu.get_barrier_semaphore()
    neighbours = ((has_l, (p - 1, d)), (has_r, (p + 1, d)), (has_b, (p, d - 1)), (has_a, (p, d + 1)))
    for cond, dev in neighbours:
        @pl.when(cond)
        def _():
            pl.semaphore_signal(barrier, 1, device_id=dev, device_id_type=MESH)
    peers = sum(cond.astype(jnp.int32) for cond, _ in neighbours)
    pl.semaphore_wait(barrier, peers)

    def copies(s):
        to_l = pltpu.make_async_remote_copy(
            field.at[s, 1, pl.ds(lo, depth), :], field.at[s, planes + 1, pl.ds(lo, depth), :],
            send_sem.at[s, 0], recv_sem.at[s, 0], device_id=(p - 1, d), device_id_type=MESH)
        to_r = pltpu.make_async_remote_copy(
            field.at[s, planes, pl.ds(lo, depth), :], field.at[s, 0, pl.ds(lo, depth), :],
            send_sem.at[s, 1], recv_sem.at[s, 1], device_id=(p + 1, d), device_id_type=MESH)
        to_b = pltpu.make_async_remote_copy(
            field.at[s, pl.ds(1, planes), pl.ds(lo, HALO), :], field.at[s, pl.ds(1, planes), pl.ds(hi, HALO), :],
            send_sem.at[s, 2], recv_sem.at[s, 2], device_id=(p, d - 1), device_id_type=MESH)
        to_a = pltpu.make_async_remote_copy(
            field.at[s, pl.ds(1, planes), pl.ds(hi - HALO, HALO), :], field.at[s, pl.ds(1, planes), pl.ds(0, HALO), :],
            send_sem.at[s, 3], recv_sem.at[s, 3], device_id=(p, d + 1), device_id_type=MESH)
        return ((to_l, has_l, has_r), (to_r, has_r, has_l), (to_b, has_b, has_a), (to_a, has_a, has_b))

    def exchange(s):
        group = copies(s)
        for copy, send, _ in group:
            @pl.when(send)
            def _():
                copy.start()
        for copy, send, recv in group:
            @pl.when(send)
            def _():
                copy.wait_send()

            @pl.when(recv)
            def _():
                copy.wait_recv()

    lane = lax.broadcasted_iota(jnp.int32, (depth, width), 1)

    def update(s, i, r0, rows, last):
        at = lo + r0
        c = field[s, i + 1, pl.ds(at, rows), :]
        zm = field[s, i + 1, pl.ds(at - 1, rows), :]
        zp = field[s, i + 1, pl.ds(at + 1, rows), :]
        xm = field[s, i, pl.ds(at, rows), :]
        xp = field[s, i + 2, pl.ds(at, rows), :]
        lanes = lane[:rows]
        ym = jnp.where(lanes == 0, 0.0, pltpu.roll(c, 1, 1))
        yp = jnp.where(lanes == width - 1, 0.0, pltpu.roll(c, width - 1, 1))
        part = pl.ds(r0, rows)
        new = (src_ref[i, part, :] + cx_ref[i, part, :] * (xm + xp) + cy_ref[i, part, :] * (ym + yp)
               + cz_ref[i, part, :] * (zm + zp)) * inv_ref[i, part, :]
        if last and turn_src:
            out_ref[i, part, :] = new
        elif last:
            out_ref[i] = new.T
        else:
            field[1 - s, i + 1, pl.ds(at, rows), :] = new

    def sweep_send(s):
        t = 1 - s
        group = copies(t)
        update(s, 0, 0, depth, False)
        update(s, planes - 1, 0, depth, False)
        for copy, send, _ in group[:2]:
            @pl.when(send)
            def _():
                copy.start()
        for i in range(1, planes - 1):
            update(s, i, 0, HALO, False)
            update(s, i, depth - HALO, HALO, False)
        for copy, send, _ in group[2:]:
            @pl.when(send)
            def _():
                copy.start()
        for i in range(1, planes - 1):
            update(s, i, HALO, depth - 2 * HALO, False)
        for copy, send, recv in group:
            @pl.when(send)
            def _():
                copy.wait_send()

            @pl.when(recv)
            def _():
                copy.wait_recv()

    exchange(0)

    def pair(k, carry):
        sweep_send(0)
        sweep_send(1)
        return carry

    lax.fori_loop(0, SWEEPS // 2 - 1, pair, 0)
    sweep_send(0)
    for i in range(planes):
        update(1, i, 0, depth, True)


def smooth_each(source, class_ids, class_radii, n_plan, n_draw, kid, turn_src):
    planes, depth, width = source.shape
    vmem = pl.BlockSpec(memory_space=pltpu.VMEM)
    smem = pl.BlockSpec(memory_space=pltpu.SMEM)
    return pl.pallas_call(
        functools.partial(filter_kernel, n_plan, n_draw, turn_src),
        out_shape=jax.ShapeDtypeStruct(source.shape, jnp.float32),
        in_specs=[vmem, vmem, smem],
        out_specs=vmem,
        scratch_shapes=[
            pltpu.VMEM((2, planes + 2, depth + 2 * HALO, width), jnp.float32),
            pltpu.VMEM(source.shape, jnp.float32),
            pltpu.VMEM(source.shape, jnp.float32),
            pltpu.VMEM(source.shape, jnp.float32),
            pltpu.VMEM(source.shape, jnp.float32),
            pltpu.VMEM(source.shape, jnp.float32),
            pltpu.SemaphoreType.DMA((2, 4)),
            pltpu.SemaphoreType.DMA((2, 4)),
        ],
        compiler_params=pltpu.CompilerParams(collective_id=kid, has_side_effects=True),
    )(source, class_ids, class_radii)


def per_device(n_plan, n_draw, design, class_ids, class_radii, sensitivity, row_patch):
    sens_t = jnp.swapaxes(sensitivity, 1, 2)
    filtered = smooth_each(design, class_ids, class_radii, n_plan, n_draw, 0, True)
    denom = jnp.tanh(jnp.float32(BETA * ETA)) + jnp.tanh(jnp.float32(BETA * (1.0 - ETA)))
    steep = jnp.tanh(BETA * (filtered - ETA))
    projected = RMIN + (1.0 - RMIN) * (jnp.tanh(jnp.float32(BETA * ETA)) + steep) / denom
    running = jnp.cumsum(jnp.power(projected, POWER), axis=1)
    totals = running[:, -1, :]
    carried = entering(totals, n_draw, False, 2)
    prefix = running + carried[:, None, :]
    cast_density = jnp.power(prefix, 1.0 / POWER)
    weighted = sens_t * jnp.power(prefix, (1.0 - POWER) / POWER)
    backward = lax.cumsum(weighted, axis=1, reverse=True)
    rests = backward[:, 0, :]
    below = entering(rests, n_draw, True, 3)
    suffix = backward + below[:, None, :]
    chained = (
        jnp.power(projected, POWER - 1.0)
        * suffix
        * (1.0 - RMIN)
        * BETA
        * (1.0 - steep * steep)
        / denom
    )
    filtered_sens_t = smooth_each(chained, class_ids, class_radii, n_plan, n_draw, 1, False)
    filtered_sens = filtered_sens_t
    cast_density = jnp.swapaxes(cast_density, 1, 2)
    depth = filtered_sens.shape[2]
    row_count = filtered_sens.shape[0] * filtered_sens.shape[1]
    tiles = lax.axis_size("plan")
    capacity = 4 * row_count // tiles
    row_data = filtered_sens.reshape(row_count, depth)
    patch_ids = row_patch.reshape(row_count)
    owners = patch_ids // PATCH_DEV
    slot_patch = patch_ids - owners * PATCH_DEV
    onehot = (owners[:, None] == jnp.arange(tiles, dtype=jnp.int32)[None, :]).astype(jnp.bfloat16)
    rows = jnp.arange(row_count, dtype=jnp.int32)
    upto = (rows[None, :] <= rows[:, None]).astype(jnp.bfloat16)
    counted = jnp.dot(upto, onehot, preferred_element_type=jnp.float32)
    ranking = jnp.sum(counted * onehot.astype(jnp.float32), axis=1).astype(jnp.int32) - 1
    position = owners * capacity + ranking
    slots = tiles * capacity
    key = 2 * PATCH_DEV
    filled = jnp.full((slots,), row_count * key + PATCH_DEV, jnp.int32).at[position].set(rows * key + slot_patch)
    source_row = filled // key
    send_ids = (filled % key).astype(jnp.float32)
    id_rows = capacity // depth
    pad_rows = (-id_rows) % 8
    table = jnp.concatenate([row_data, jnp.zeros((1, depth), jnp.float32), send_ids.reshape(slots // depth, depth)])
    chunk_rows = source_row.reshape(tiles, capacity)
    id_index = row_count + 1 + jnp.arange(tiles * id_rows, dtype=jnp.int32).reshape(tiles, id_rows)
    pad_index = jnp.full((tiles, pad_rows), row_count, jnp.int32)
    index = jnp.concatenate([chunk_rows, id_index, pad_index], axis=1).reshape(-1)
    sendbuf = jnp.take(table, index, axis=0).reshape(tiles, capacity + id_rows + pad_rows, depth)
    arrived_all = lax.all_to_all(sendbuf, "plan", split_axis=0, concat_axis=0, tiled=True)
    arrived = arrived_all[:, :capacity, :]
    arrived_ids = arrived_all[:, capacity:capacity + id_rows, :]
    picks = (
        jnp.arange(PATCH_DEV, dtype=jnp.int32)[:, None] == arrived_ids.reshape(1, tiles * capacity).astype(jnp.int32)
    ).astype(jnp.float32)
    summed = jnp.dot(picks, arrived.reshape(tiles * capacity, depth), precision=lax.Precision.HIGH,
                     preferred_element_type=jnp.float32)
    patch_sens = 0.25 * summed
    return (cast_density, filtered_sens, patch_sens)


def solution(mesh):
    in_specs = (
        P("plan", None, "draw"),
        P("plan", None, "draw"),
        P(),
        P("plan", None, "draw"),
        P("plan", "draw", None),
    )
    out_specs = (P("plan", None, "draw"), P("plan", None, "draw"), P("plan", "draw"))
    return jax.shard_map(
        functools.partial(per_device, mesh.shape["plan"], mesh.shape["draw"]),
        mesh=mesh, in_specs=in_specs, out_specs=out_specs, check_vma=False
    )
```
